512 devices in a mesh: sec: 64 (over y, z), term: 8 (over x, core).
Axes of the slice: x: 4, y: 8, z: 8, core: 2. Of those that a mesh axis runs over, the one named last changes fastest.
Arguments:
- psi: bfloat16 [64, 3, 256, 256], P('sec'), may hold values from -6 to 6
- left_ops: bfloat16 [64, 64, 256, 256], P('term', 'sec'), may hold values from -0.375 to 0.375
- right_ops: bfloat16 [64, 64, 256, 256], P('term', 'sec'), may hold values from -0.046875 to 0.046875
- left_dims: int32 [64], replicated, may hold values from 1 to 256, 8192 in all
- right_dims: int32 [64], replicated, may hold values from 1 to 256, 8192 in all
Outputs:
- new_state: bfloat16 [64, 3, 256, 256], P('sec')
- kept: float32 [64, 256, 256], P('sec')
- energy: float32 [], replicated
The draws below stay inside these ranges and needn't reach their ends.
Inputs may be any that keep to these rules, and one draw needn't show every extreme that they name: `left_dims`: the 64 sector dimensions sum to 8192 and the largest is exactly 256. `right_dims`: the 64 sector dimensions sum to 8192 and the largest is exactly 256.
All inputs are finite; a program needn't handle non-finite values.
Results may differ from the reference program's by a relative error of at most 0.0058.
Values may be sent and summed in bfloat16 or wider, within the bound.
A program may use at most 64 MiB of HBM per device.

```python
import math
import jax
import jax.numpy as jnp
import numpy as np
from jax import lax

CAP = 256
NK = 3
SIGN_STEPS = 6
NS = 64
NTERM = 64


def levels(own_key, shape, split, least, top_value):
    level = 1.0
    for position, shards_of in split:
        steps = jax.random.uniform(jax.random.fold_in(jax.random.fold_in(own_key, 6), position), (shards_of,), jnp.float32, least / len(split), top_value / len(split))
        level = level * jnp.repeat(jnp.exp(steps), shape[position] // shards_of).reshape((-1,) + (1,) * (len(shape) - 1 - position))
    return level


def profile(count, total, bound, lean):
    portions = [(1 << 20) // math.isqrt(standing ** lean) + 1 for standing in range(2, count + 1)]
    spare, counts = total - bound - (count - 1), [1] * (count - 1)
    while spare > 0:
        candidates = [i for i in range(count - 1) if counts[i] < bound]
        mass, remaining = sum([portions[i] for i in candidates]), spare
        for i in candidates:
            extra = min(bound - counts[i], max(1, remaining * portions[i] // mass), spare)
            counts[i] = counts[i] + extra
            spare = spare - extra
    return np.array([bound] + counts)


def uneven_parts(stream_key, amount, total, limit, lean):
    if amount == 2:
        one = jax.random.randint(stream_key, (), max(1, total - limit), min(limit, total - 1) + 1)
        return jnp.stack([one, total - one])
    tallies = jnp.asarray(profile(amount, total, limit, lean), jnp.int32)
    couples = (amount - 1) // 2
    giver, taker = tallies[1:1 + 2 * couples:2], tallies[2:2 + 2 * couples:2]
    slack = jnp.minimum(giver - 1, limit - taker)
    moved = jax.random.randint(jax.random.fold_in(stream_key, 1), (couples,), 0, 1 << 20) % (slack + 1)
    tallies = tallies.at[1:1 + 2 * couples:2].set(giver - moved).at[2:2 + 2 * couples:2].set(taker + moved)
    return tallies[jax.random.permutation(jax.random.fold_in(stream_key, 2), amount)]


def bell_draw(stream_key, dims, scale, most, split=(), kind=jnp.bfloat16):
    entries = scale * jax.random.normal(stream_key, dims, jnp.float32)
    if split:
        entries = entries * levels(stream_key, dims, split, -0.22, 0.18)
    return jnp.clip(entries, -most, most).astype(kind)


def setup_inputs(seed: int = 0) -> dict:
    seeds = jax.random.split(jax.random.key(seed), 6)
    return {
        "psi": bell_draw(seeds[0], (NS, NK, CAP, CAP), 1.0, 6.0, ((0, 64),)),
        "left_ops": bell_draw(seeds[1], (NTERM, NS, CAP, CAP), CAP ** -0.5, 0.375, ((0, 8), (1, 64))),
        "right_ops": bell_draw(seeds[2], (NTERM, NS, CAP, CAP), (CAP * NTERM) ** -0.5, 0.046875, ((0, 8), (1, 64))),
        "left_dims": uneven_parts(seeds[3], NS, NS * CAP // 2, CAP, 2).astype(jnp.int32),
        "right_dims": uneven_parts(seeds[4], NS, NS * CAP // 2, CAP, 2).astype(jnp.int32),
    }


noise_weight = 0.5
highest = lax.Precision.HIGHEST

def symmetric(blocks):
    widened = blocks.astype(jnp.float32)
    return (widened + jnp.swapaxes(widened, -1, -2)).astype(jnp.bfloat16)

def subspace(a11, h11, a12, a22, h12, h22):
    quad_a = a11 * a22 - a12 * a12
    quad_b = h11 * a22 + h22 * a11 - 2.0 * h12 * a12
    quad_c = h11 * h22 - h12 * h12
    lowest = (quad_b - jnp.sqrt(jnp.maximum(quad_b * quad_b - 4.0 * quad_a * quad_c, 0.0))) / (2.0 * quad_a)
    ratio = (lowest * a11 - h11) / (h12 - lowest * a12)
    scale = lax.rsqrt(a11 + 2.0 * ratio * a12 + ratio * ratio * a22)
    return (lowest, scale, ratio * scale)

def sign_projector(density, live_count):
    order_size = density.shape[-1]
    identity = jnp.eye(order_size, dtype=jnp.float32)
    mean_value = jnp.trace(density, axis1=-2, axis2=-1) / live_count
    shifted = density - mean_value[:, None, None] * identity
    frobenius = jnp.sqrt(lax.optimization_barrier(jnp.sum(shifted * shifted, axis=(1, 2), keepdims=True)))
    current = shifted / frobenius
    for repeat in range(SIGN_STEPS):
        squared = jnp.matmul(current, current, precision=highest)
        cubed_term = jnp.matmul(squared, current, precision=highest)
        current = 1.5 * current - 0.5 * cubed_term
    return 0.5 * (identity + current)

def reference(psi, left_ops, right_ops, left_dims, right_dims):
    states = jnp.arange(CAP, dtype=jnp.int32)
    sectors = jnp.arange(NS, dtype=jnp.int32)
    offsets = jnp.arange(NK, dtype=jnp.int32)
    paired = sectors[:, None] + offsets[None, :]
    safe = jnp.minimum(paired, NS - 1)
    select = paired[:, :, None] == sectors[None, None, :]
    pair_dims = lax.optimization_barrier(jnp.sum(jnp.where(select, left_dims[None, None, :], 0), axis=2))
    left_live = (states[None, None, :] < pair_dims[:, :, None]).astype(jnp.float32)
    right_live = (states[None, :] < right_dims[:, None]).astype(jnp.float32)
    mask = left_live[:, :, :, None] * right_live[:, None, None, :]
    vector = psi * mask.astype(jnp.bfloat16)

    def images_of(sector, blocks):
        lefts = symmetric(jnp.take(left_ops, safe[sector], axis=1))
        rights = symmetric(lax.dynamic_index_in_dim(right_ops, sector, 1, keepdims=False))
        images = jnp.einsum('tkij,kjl->tkil', lefts.astype(jnp.float32), blocks.astype(jnp.float32)).astype(jnp.bfloat16)
        return (images, rights)

    def apply_all(blocks_all):

        def one_sector(packed):
            sector, blocks, block_mask = packed
            images, rights = images_of(sector, blocks)
            return jnp.einsum('tkil,tlm->kim', images.astype(jnp.float32), rights.astype(jnp.float32)) * block_mask
        return lax.map(one_sector, (sectors, blocks_all, mask))
    vector_wide = vector.astype(jnp.float32)
    first = apply_all(vector)
    a11 = jnp.sum(vector_wide * vector_wide)
    h11 = jnp.sum(vector_wide * first)
    correction = (first - h11 / a11 * vector_wide).astype(jnp.bfloat16)
    corr_wide = correction.astype(jnp.float32)
    second = apply_all(correction)
    a12 = jnp.sum(vector_wide * corr_wide)
    a22 = jnp.sum(corr_wide * corr_wide)
    h12 = jnp.sum(vector_wide * second)
    h22 = jnp.sum(corr_wide * second)
    energy, first_coef, second_coef = subspace(a11, h11, a12, a22, h12, h22)
    new_state = (first_coef * vector_wide + second_coef * corr_wide).astype(jnp.bfloat16)

    def piece_of(packed):
        sector, blocks_one, blocks_two, state_blocks, row_live = packed
        images_one, rights = images_of(sector, blocks_one)
        images_two, rights = images_of(sector, blocks_two)
        weighted = ((first_coef * images_one.astype(jnp.float32) + second_coef * images_two.astype(jnp.float32)) * row_live[None, :, :, None]).astype(jnp.bfloat16)
        weighted_wide = weighted.astype(jnp.float32)
        noise_part = jnp.einsum('tkil,tkjl->kij', weighted_wide, weighted_wide)
        state_wide = state_blocks.astype(jnp.float32)
        own_part = jnp.einsum('kil,kjl->kij', state_wide, state_wide)
        return own_part + noise_weight / NTERM * noise_part
    pieces = lax.map(piece_of, (sectors, vector, correction, new_state, left_live))
    density = pieces[:, 0]
    for offset in range(1, NK):
        density = density + jnp.pad(pieces[:NS - offset, offset], ((offset, 0), (0, 0), (0, 0)))
    kept = sign_projector(density, left_dims.astype(jnp.float32))
    return (new_state, kept, energy)
```

```python
import functools

import jax
import jax.numpy as jnp
from jax import lax
from jax.experimental import pallas as pl
from jax.experimental.pallas import tpu as pltpu
from jax.sharding import PartitionSpec as P

SIGN_STEPS = 6
ZSIZE = 8
CORES = 2
NOISE_WEIGHT = 0.5
MESH = pl.DeviceIdType.MESH
F32 = jnp.float32
BF16 = jnp.bfloat16


def dot(a, b):
    return jnp.dot(a, b, preferred_element_type=F32)


def dot_t(a, b):
    return lax.dot_general(a, b, (((1,), (1,)), ((), ())), preferred_element_type=F32)


def fold(value):
    half = value.shape[1] // 2
    row = jnp.sum(value, axis=0, keepdims=True)
    return row[:, :half] + row[:, half:]


def kernel(
    sizes,
    left_dims, right_dims, psi, left, right,
    new_state, kept, energy,
    sl0, sr0, sl1, sr1, pack_l, pack_r, got_l, got_r, got_psi,
    vec, cor, img_a, img_b, acc, nacc, half_a, half_n, core_a, core_n, part_a, part_n,
    sums, totals, ns_mine, ns_got, piece_out, piece_in, dens,
    pack_send, pack_recv, one_send, one_recv, x_send, x_recv, s_send, s_recv,
):
    ns, zs, tg, terms, width = sizes
    ys, xs = ns // zs, tg // CORES
    half, quarter = width // 2, width // 2 // xs
    me, lane = lax.axis_index("sec"), lax.axis_index("term")
    x, c = lax.div(lane, CORES), lax.rem(lane, CORES)
    y, z = lax.div(me, zs), lax.rem(me, zs)
    up, down = lax.rem(me + 1, ns), lax.rem(me + ns - 1, ns)
    partner = lane + 1 - 2 * c
    lanes_x = [lax.rem(x + d, xs) * CORES + c for d in range(1, xs)]
    in_x = [lax.rem(x + d, xs) for d in range(1, xs)]

    def send(src, dst, ssem, rsem, sec, term):
        return pltpu.make_async_remote_copy(
            src_ref=src, dst_ref=dst, send_sem=ssem, recv_sem=rsem,
            device_id=(sec, term), device_id_type=MESH,
        )

    barrier = pltpu.get_barrier_semaphore()
    groups = [
        [((me, lax.rem(lane + d, tg)), lax.rem(lane + d, tg)) for d in range(1, tg)],
        [((y * zs + lax.rem(z + d, zs), lane), lax.rem(z + d, zs)) for d in range(1, zs)],
        [((lax.rem(y + d, ys) * zs + z, lane), lax.rem(y + d, ys)) for d in range(1, ys)],
    ]
    places = [lane, z, y]
    greeted = [peer for group in groups for peer, _ in group] + [(up, lane), (down, lane)]
    for peer in greeted:
        pl.semaphore_signal(barrier, inc=1, device_id=peer, device_id_type=MESH)

    row_h = lax.broadcasted_iota(jnp.int32, (half, half), 0)
    col_h = lax.broadcasted_iota(jnp.int32, (half, half), 1)

    def prepare(t, raw, sym, pack):
        wide = raw[t].astype(F32)
        whole = (wide + wide.T).astype(BF16)
        sym[t] = whole
        again = whole.astype(F32)
        low, high = again[:half, :half], again[half:, half:]
        pack[t, :half] = whole[:half, half:]
        pack[t, half:width] = jnp.where(row_h <= col_h, low, high).astype(BF16)
        diag = jnp.sum(jnp.where(row_h == col_h, high, 0.0), axis=0, keepdims=True)
        pack[t, width:] = jnp.broadcast_to(diag, (16, half)).astype(BF16)

    def restore(t, pack, sym):
        corner = pack[t, :half].astype(F32)
        mixed = pack[t, half:width].astype(F32)
        diag = pack[t, width:].astype(F32)[0:1]
        turned = mixed.T
        sym[t, :half, :half] = jnp.where(row_h <= col_h, mixed, turned).astype(BF16)
        sym[t, :half, half:] = pack[t, :half]
        sym[t, half:, :half] = corner.T.astype(BF16)
        lower = jnp.where(row_h == col_h, jnp.broadcast_to(diag, (half, half)), turned)
        sym[t, half:, half:] = jnp.where(row_h > col_h, mixed, lower).astype(BF16)

    def ops_copies(t):
        return (
            send(pack_l.at[t], got_l.at[t], pack_send.at[0, t], pack_recv.at[0, t], down, lane),
            send(pack_r.at[t], got_r.at[t], pack_send.at[1, t], pack_recv.at[1, t], up, lane),
        )

    prepare(0, left, sl0, pack_l)
    prepare(0, right, sr0, pack_r)
    pl.semaphore_wait(barrier, len(greeted))
    psi_copy = send(psi.at[2], got_psi, one_send.at[0], one_recv.at[0], up, lane)
    psi_copy.start()

    @pl.loop(1, terms)
    def _(t):
        prepare(t, left, sl0, pack_l)
        prepare(t, right, sr0, pack_r)
        for copy in ops_copies(t - 1):
            copy.start()

    inside = me + 1 < ns
    rows_own = left_dims[me]
    rows_next = jnp.where(inside, left_dims[up], 0)
    cols_own = right_dims[me]
    cols_last = jnp.where(me >= 1, right_dims[down], 0)
    live_rows = [rows_own, rows_next, rows_next]
    live_cols = [cols_own, cols_own, cols_last]

    def mask_of(k, first_row, count):
        row = lax.broadcasted_iota(jnp.int32, (count, width), 0) + first_row
        col = lax.broadcasted_iota(jnp.int32, (count, width), 1)
        return (row < live_rows[k]) & (col < live_cols[k])

    for k in range(2):
        vec[k] = jnp.where(mask_of(k, 0, width), psi[k].astype(F32), 0.0).astype(BF16)
    for copy in ops_copies(terms - 1):
        copy.start()

    def part_own(t, blocks, images):
        image = dot(sl0[t], blocks[0]).astype(BF16)
        images[t, 0] = image
        acc[0] += dot(image, sr0[t])

    def part_near(t, blocks, images):
        one = dot(sl1[t], blocks[1]).astype(BF16)
        two = dot(sl1[t], blocks[2]).astype(BF16)
        images[t, 1] = one
        images[t, 2] = two
        acc[1] += dot(one, sr0[t])
        acc[2] += dot(two, sr1[t])

    acc[...] = jnp.zeros_like(acc)

    @pl.loop(0, terms)
    def _(t):
        part_own(t, vec, img_a)

    psi_copy.wait_recv()
    vec[2] = jnp.where(mask_of(2, 0, width), got_psi[...].astype(F32), 0.0).astype(BF16)

    @pl.loop(0, terms)
    def _(t):
        for copy in ops_copies(t):
            copy.wait_recv()
        restore(t, got_l, sl1)
        restore(t, got_r, sr1)
        part_near(t, vec, img_a)

    def scalar_round(rnd, stage):
        copies = []
        for d, (peer, _) in enumerate(groups[stage]):
            copies.append(send(
                sums.at[rnd, stage, places[stage]], sums.at[rnd, stage, places[stage]],
                s_send.at[rnd, stage, d], s_recv.at[rnd, stage, places[stage]], *peer,
            ))
        return copies

    def scalar_wait(rnd, stage, copies):
        for d, (peer, place) in enumerate(groups[stage]):
            send(
                sums.at[rnd, stage, place], sums.at[rnd, stage, place],
                s_send.at[rnd, stage, d], s_recv.at[rnd, stage, place], *peer,
            ).wait_recv()
        total = sums[rnd, stage, 0]
        for i in range(1, len(groups[stage]) + 1):
            total = total + sums[rnd, stage, i]
        return total

    waits = []

    def start_all(copies):
        for copy in copies:
            copy.start()
        waits.extend(copies)

    def put_rows(rnd, rows):
        rows = rows + [jnp.zeros((8 - len(rows), half), F32)]
        sums[rnd, 0, lane] = jnp.concatenate(rows, axis=0)

    mine = pl.multiple_of(c * half, half)
    other = pl.multiple_of((1 - c) * half, half)
    own_row = pl.multiple_of(c * half + x * quarter, quarter)
    share = pl.ds(pl.multiple_of(x * quarter, quarter), quarter)

    def x_scatter(src, dst, base):
        return [
            send(
                src.at[:, pl.ds(pl.multiple_of(in_x[i] * quarter, quarter), quarter), :],
                dst.at[x], x_send.at[base, i], x_recv.at[base, x], me, lanes_x[i],
            )
            for i in range(xs - 1)
        ]

    def x_wait(src, dst, base):
        for i in range(xs - 1):
            send(
                src.at[:, share, :], dst.at[in_x[i]],
                x_send.at[base, i], x_recv.at[base, in_x[i]], me, lanes_x[i],
            ).wait_recv()

    def rows_at(ref, index):
        start = pl.multiple_of(c * half + index * quarter, quarter)
        return ref.at[..., pl.ds(start, quarter), :]

    def x_gather(ref, base):
        return [
            send(
                rows_at(ref, x), rows_at(ref, x), x_send.at[base, i], x_recv.at[base, x],
                me, lanes_x[i],
            )
            for i in range(xs - 1)
        ]

    def x_gather_wait(ref, base):
        for i in range(xs - 1):
            send(
                rows_at(ref, in_x[i]), rows_at(ref, in_x[i]), x_send.at[base, i],
                x_recv.at[base, in_x[i]], me, lanes_x[i],
            ).wait_recv()

    def core_gather(ref, slot):
        piece = ref.at[..., pl.ds(mine, half), :]
        return send(piece, piece, one_send.at[slot], one_recv.at[slot], me, partner)

    def core_gather_wait(ref, slot):
        piece = ref.at[..., pl.ds(other, half), :]
        send(piece, piece, one_send.at[slot], one_recv.at[slot], me, partner).wait_recv()

    h11 = a11 = jnp.zeros((1, half), F32)
    for k in range(3):
        wide = vec[k].astype(F32)
        h11 = h11 + fold(wide * acc[k])
        a11 = a11 + fold(wide * wide)
    put_rows(0, [h11, a11])
    core_copy = send(
        acc.at[:, pl.ds(other, half), :], core_a, one_send.at[1], one_recv.at[1], me, partner
    )
    start_all([core_copy])
    start_all(scalar_round(0, 0))
    core_copy.wait_recv()
    half_a[...] = acc[:, pl.ds(mine, half), :] + core_a[...]
    sums[0, 1, z] = scalar_wait(0, 0, None)
    start_all(x_scatter(half_a, part_a, 0))
    start_all(scalar_round(0, 1))
    sums[0, 2, y] = scalar_wait(0, 1, None)
    x_wait(half_a, part_a, 0)
    part_a[x] = half_a[:, share, :]
    start_all(scalar_round(0, 2))
    shard = part_a[0]
    for i in range(1, xs):
        shard = shard + part_a[i]
    total = scalar_wait(0, 2, None)
    h11 = jnp.sum(total[0:1], axis=1, keepdims=True)
    a11 = jnp.sum(total[1:2], axis=1, keepdims=True) * (1.0 / tg)
    level = h11 / a11
    for k in range(3):
        held = vec[k, pl.ds(own_row, quarter), :].astype(F32)
        inside_k = jnp.where(mask_of(k, own_row, quarter), shard[k], 0.0)
        cor[k, pl.ds(own_row, quarter), :] = (inside_k - level * held).astype(BF16)
    start_all(x_gather(cor, 1))
    x_gather_wait(cor, 1)
    core_copy_two = core_gather(cor, 2)
    start_all([core_copy_two])
    core_copy.wait_send()
    acc[...] = jnp.zeros_like(acc)
    core_gather_wait(cor, 2)

    @pl.loop(0, terms)
    def _(t):
        part_own(t, cor, img_b)
        part_near(t, cor, img_b)

    a12 = a22 = h12 = h22 = jnp.zeros((1, half), F32)
    for k in range(3):
        wide, corr = vec[k].astype(F32), cor[k].astype(F32)
        summed = acc[k]
        a12 = a12 + fold(wide * corr)
        a22 = a22 + fold(corr * corr)
        h12 = h12 + fold(wide * summed)
        h22 = h22 + fold(corr * summed)
    put_rows(1, [a12, a22, h12, h22])
    start_all(scalar_round(1, 0))
    sums[1, 1, z] = scalar_wait(1, 0, None)
    start_all(scalar_round(1, 1))
    sums[1, 2, y] = scalar_wait(1, 1, None)
    start_all(scalar_round(1, 2))
    total = scalar_wait(1, 2, None)
    whole = jnp.sum(total, axis=1, keepdims=True)
    a12, a22 = whole[0:1] * (1.0 / tg), whole[1:2] * (1.0 / tg)
    h12, h22 = whole[2:3], whole[3:4]
    quad_a = a11 * a22 - a12 * a12
    quad_b = h11 * a22 + h22 * a11 - 2.0 * h12 * a12
    quad_c = h11 * h22 - h12 * h12
    lowest = (quad_b - jnp.sqrt(jnp.maximum(quad_b * quad_b - 4.0 * quad_a * quad_c, 0.0))) / (
        2.0 * quad_a
    )
    ratio = (lowest * a11 - h11) / (h12 - lowest * a12)
    first_coef = lax.rsqrt(a11 + 2.0 * ratio * a12 + ratio * ratio * a22)
    second_coef = ratio * first_coef
    energy[...] = lowest

    for k in range(3):
        ns_mine[k] = (first_coef * vec[k].astype(F32) + second_coef * cor[k].astype(F32)).astype(BF16)
    nacc[...] = jnp.zeros_like(nacc)

    @pl.loop(0, terms)
    def _(t):
        for k in range(3):
            row = lax.broadcasted_iota(jnp.int32, (width, width), 0)
            mixed = first_coef * img_a[t, k].astype(F32) + second_coef * img_b[t, k].astype(F32)
            weighted = jnp.where(row < live_rows[k], mixed, 0.0).astype(BF16)
            nacc[min(k, 1)] += dot_t(weighted, weighted)

    ns_copy = send(ns_mine.at[2], ns_got, one_send.at[3], one_recv.at[3], down, lane)
    core_noise = send(
        nacc.at[:, pl.ds(other, half), :], core_n, one_send.at[4], one_recv.at[4], me, partner
    )
    new_state[0] = ns_mine[0]
    new_state[1] = ns_mine[1]
    start_all([core_noise])
    own = [dot_t(ns_mine[k, pl.ds(own_row, quarter), :], ns_mine[k]) for k in range(3)]
    core_noise.wait_recv()
    half_n[...] = nacc[:, pl.ds(mine, half), :] + core_n[...]
    start_all([ns_copy])
    start_all(x_scatter(half_n, part_n, 2))
    x_wait(half_n, part_n, 2)
    part_n[x] = half_n[:, share, :]
    noise = part_n[0]
    for i in range(1, xs):
        noise = noise + part_n[i]
    scale = NOISE_WEIGHT / (terms * tg)
    piece_out[...] = own[1] + own[2] + scale * noise[1]
    piece_copy = send(piece_out, piece_in, one_send.at[5], one_recv.at[5], up, lane)
    start_all([piece_copy])
    stay = own[0] + scale * noise[0]
    piece_copy.wait_recv()
    dens[pl.ds(own_row, quarter), :] = stay + piece_in[...]
    start_all(x_gather(dens, 3))
    x_gather_wait(dens, 3)
    dens_copy = core_gather(dens, 6)
    start_all([dens_copy])
    ns_copy.wait_recv()
    new_state[2] = ns_got[...]
    core_gather_wait(dens, 6)

    row = lax.broadcasted_iota(jnp.int32, (width, width), 0)
    col = lax.broadcasted_iota(jnp.int32, (width, width), 1)
    identity = jnp.where(row == col, 1.0, 0.0).astype(F32)
    density = dens[...]
    trace = jnp.sum(jnp.sum(density * identity, axis=0, keepdims=True), axis=1, keepdims=True)
    count = jnp.broadcast_to(rows_own, (1, 1)).astype(F32)
    shifted = density - (trace / count) * identity
    square = jnp.sum(jnp.sum(shifted * shifted, axis=0, keepdims=True), axis=1, keepdims=True)
    kept[...] = shifted / jnp.sqrt(square)

    @pl.loop(0, SIGN_STEPS)
    def _(step):
        current = kept[...]
        squared = jnp.dot(current, current, precision=lax.Precision.HIGHEST, preferred_element_type=F32)
        cubed = jnp.dot(squared, current, precision=lax.Precision.HIGHEST, preferred_element_type=F32)
        kept[...] = 1.5 * current - 0.5 * cubed

    kept[...] = 0.5 * (identity + kept[...])

    psi_copy.wait_send()

    @pl.loop(0, terms)
    def _(t):
        for copy in ops_copies(t):
            copy.wait_send()

    for copy in waits:
        if copy is not core_copy:
            copy.wait_send()


def per_device(zs, ns, tg, psi, left_ops, right_ops, left_dims, right_dims):
    terms, width = left_ops.shape[0], left_ops.shape[-1]
    half, xs = width // 2, tg // CORES
    quarter, ys = half // xs, ns // zs
    most = max(tg, zs, ys)
    vmem, smem = pl.BlockSpec(memory_space=pltpu.VMEM), pl.BlockSpec(memory_space=pltpu.SMEM)
    dma = pltpu.SemaphoreType.DMA
    state, kept, energy = pl.pallas_call(
        functools.partial(kernel, (ns, zs, tg, terms, width)),
        out_shape=(
            jax.ShapeDtypeStruct((3, width, width), BF16),
            jax.ShapeDtypeStruct((width, width), F32),
            jax.ShapeDtypeStruct((1, 1), F32),
        ),
        in_specs=[smem, smem, vmem, vmem, vmem],
        out_specs=(vmem, vmem, vmem),
        scratch_shapes=[pltpu.VMEM((terms, width, width), BF16)] * 4
        + [pltpu.VMEM((terms, width + 16, half), BF16)] * 4
        + [
            pltpu.VMEM((width, width), BF16),
            pltpu.VMEM((3, width, width), BF16),
            pltpu.VMEM((3, width, width), BF16),
            pltpu.VMEM((terms, 3, width, width), BF16),
            pltpu.VMEM((terms, 3, width, width), BF16),
            pltpu.VMEM((3, width, width), F32),
            pltpu.VMEM((2, width, width), F32),
            pltpu.VMEM((3, half, width), F32),
            pltpu.VMEM((2, half, width), F32),
            pltpu.VMEM((3, half, width), F32),
            pltpu.VMEM((2, half, width), F32),
            pltpu.VMEM((xs, 3, quarter, width), F32),
            pltpu.VMEM((xs, 2, quarter, width), F32),
            pltpu.VMEM((2, 3, most, 8, half), F32),
            pltpu.VMEM((8, half), F32),
            pltpu.VMEM((3, width, width), BF16),
            pltpu.VMEM((width, width), BF16),
            pltpu.VMEM((quarter, width), F32),
            pltpu.VMEM((quarter, width), F32),
            pltpu.VMEM((width, width), F32),
            dma((2, terms)),
            dma((2, terms)),
            dma((7,)),
            dma((7,)),
            dma((4, xs)),
            dma((4, xs)),
            dma((2, 3, most)),
            dma((2, 3, most)),
        ],
        compiler_params=pltpu.CompilerParams(
            collective_id=0, has_side_effects=True, vmem_limit_bytes=48 << 20
        ),
    )(left_dims, right_dims, psi[0], left_ops[:, 0], right_ops[:, 0])
    return state[None], kept[None], energy[0, 0]


def solution(mesh):
    ns, tg = mesh.shape["sec"], mesh.shape["term"]
    zs = ZSIZE if ns % ZSIZE == 0 and ns > ZSIZE else 2
    in_specs = (
        P("sec", None, None, None),
        P("term", "sec", None, None),
        P("term", "sec", None, None),
        P(),
        P(),
    )
    out_specs = (P("sec", None, None, None), P("sec", None, None), P())
    return jax.shard_map(
        functools.partial(per_device, zs, ns, tg),
        mesh=mesh, in_specs=in_specs, out_specs=out_specs, check_vma=False,
    )
```

```python
import functools

import jax
import jax.numpy as jnp
from jax import lax
from jax.experimental import pallas as pl
from jax.experimental.pallas import tpu as pltpu
from jax.sharding import PartitionSpec as P

SIGN_STEPS = 6
ZSIZE = 8
CORES = 2
NOISE_WEIGHT = 0.5
MESH = pl.DeviceIdType.MESH
F32 = jnp.float32
BF16 = jnp.bfloat16


def dot(a, b):
    return jnp.dot(a, b, preferred_element_type=F32)


def dot_t(a, b):
    return lax.dot_general(a, b, (((1,), (1,)), ((), ())), preferred_element_type=F32)


def halves(value):
    high = value.astype(BF16)
    return high, (value - high.astype(F32)).astype(BF16)


def dot_wide(a, b):
    (ah, al), (bh, bl) = a, b
    return dot(ah, bh) + (dot(ah, bl) + dot(al, bh))


def fold(value):
    half = value.shape[1] // 2
    row = jnp.sum(value, axis=0, keepdims=True)
    return row[:, :half] + row[:, half:]


def kernel(
    sizes,
    left_dims_hbm, right_dims_hbm, psi_hbm, left_hbm, right_hbm,
    new_state, kept, energy,
    left_dims, right_dims, psi, left, right,
    sl0, sr0, sl1, sr1, pack_l, pack_r, got_l, got_r, got_psi,
    vec, cor, img_a, img_b, acc, acc_b, core_a, half_a, part_a,
    n_one, n_two, mats, core_m, half_m, part_m, hop_out, hop_in, folded,
    sums, ns_two, ns_got,
    in_sem, pack_send, pack_recv, one_send, one_recv, c_send, c_recv, x_send, x_recv, s_send, s_recv,
):
    ns, zs, tg, terms, width = sizes
    ys, xs = ns // zs, tg // CORES
    half = width // 2
    me, lane = lax.axis_index("sec"), lax.axis_index("term")
    x, c = lax.div(lane, CORES), lax.rem(lane, CORES)
    y, z = lax.div(me, zs), lax.rem(me, zs)
    up, down = lax.rem(me + 1, ns), lax.rem(me + ns - 1, ns)
    partner = lane + 1 - 2 * c
    far_first = sorted(range(1, xs), key=lambda d: -min(d, xs - d))
    order = [lax.rem(x + d, xs) for d in far_first] + [x]

    def send(src, dst, ssem, rsem, sec, term):
        return pltpu.make_async_remote_copy(
            src_ref=src, dst_ref=dst, send_sem=ssem, recv_sem=rsem,
            device_id=(sec, term), device_id_type=MESH,
        )

    barrier = pltpu.get_barrier_semaphore()
    groups = [
        [((me, lax.rem(lane + d, tg)), lax.rem(lane + d, tg)) for d in range(1, tg)],
        [((y * zs + lax.rem(z + d, zs), lane), lax.rem(z + d, zs)) for d in range(1, zs)],
        [((lax.rem(y + d, ys) * zs + z, lane), lax.rem(y + d, ys)) for d in range(1, ys)],
    ]
    places = [lane, z, y]
    greeted = [peer for group in groups for peer, _ in group] + [(up, lane), (down, lane)]
    for peer in greeted:
        pl.semaphore_signal(barrier, inc=1, device_id=peer, device_id_type=MESH)

    def load_ops(t):
        return (
            pltpu.make_async_copy(left_hbm.at[t], left.at[t], in_sem.at[0, t]),
            pltpu.make_async_copy(right_hbm.at[t], right.at[t], in_sem.at[1, t]),
        )

    loads = [
        pltpu.make_async_copy(psi_hbm, psi, in_sem.at[2, 0]),
        pltpu.make_async_copy(left_dims_hbm, left_dims, in_sem.at[2, 1]),
        pltpu.make_async_copy(right_dims_hbm, right_dims, in_sem.at[3, 0]),
    ]
    for copy in load_ops(0):
        copy.start()
    for copy in loads:
        copy.start()
    for t in range(1, terms):
        for copy in load_ops(t):
            copy.start()

    row_h = lax.broadcasted_iota(jnp.int32, (half, half), 0)
    col_h = lax.broadcasted_iota(jnp.int32, (half, half), 1)

    def prepare(t, raw, sym, pack):
        wide = raw[t].astype(F32)
        whole = (wide + wide.T).astype(BF16)
        sym[t] = whole
        again = whole.astype(F32)
        low, high = again[:half, :half], again[half:, half:]
        pack[t, :half] = whole[:half, half:]
        pack[t, half:width] = jnp.where(row_h <= col_h, low, high).astype(BF16)
        diag = jnp.sum(jnp.where(row_h == col_h, high, 0.0), axis=0, keepdims=True)
        pack[t, width:] = jnp.broadcast_to(diag, (16, half)).astype(BF16)

    def restore(t, pack, sym):
        corner = pack[t, :half].astype(F32)
        mixed = pack[t, half:width].astype(F32)
        diag = pack[t, width:].astype(F32)[0:1]
        turned = mixed.T
        sym[t, :half, :half] = jnp.where(row_h <= col_h, mixed, turned).astype(BF16)
        sym[t, :half, half:] = pack[t, :half]
        sym[t, half:, :half] = corner.T.astype(BF16)
        lower = jnp.where(row_h == col_h, jnp.broadcast_to(diag, (half, half)), turned)
        sym[t, half:, half:] = jnp.where(row_h > col_h, mixed, lower).astype(BF16)

    def ops_copies(t):
        return (
            send(pack_l.at[t], got_l.at[t], pack_send.at[0, t], pack_recv.at[0, t], down, lane),
            send(pack_r.at[t], got_r.at[t], pack_send.at[1, t], pack_recv.at[1, t], up, lane),
        )

    def prepare_both(t):
        for copy in load_ops(t):
            copy.wait()
        prepare(t, left, sl0, pack_l)
        prepare(t, right, sr0, pack_r)

    waits = []

    def start(*copies):
        for copy in copies:
            copy.start()
        waits.extend(copies)

    def rows(ref, first, count):
        return ref.at[..., pl.ds(pl.multiple_of(first, count), count), :]

    def gather_start(ref, slot):
        hr, qr = ref.shape[-2] // 2, ref.shape[-2] // 2 // xs
        own = rows(ref, c * hr + x * qr, qr)
        for i, d in enumerate(far_first):
            start(send(own, own, x_send.at[slot, i], x_recv.at[slot, x], me, order[i] * CORES + c))
        start(send(own, own, c_send.at[slot, x], c_recv.at[slot, x], me, partner))

    def gather_pass(ref, slot):
        hr, qr = ref.shape[-2] // 2, ref.shape[-2] // 2 // xs
        for i in reversed(range(len(far_first))):
            piece = rows(ref, c * hr + order[i] * qr, qr)
            send(
                piece, piece, x_send.at[slot, i], x_recv.at[slot, order[i]], me, order[i] * CORES + c
            ).wait_recv()
            start(send(piece, piece, c_send.at[slot, order[i]], c_recv.at[slot, order[i]], me, partner))

    def gather_end(ref, slot):
        hr, qr = ref.shape[-2] // 2, ref.shape[-2] // 2 // xs
        for i in range(xs):
            piece = rows(ref, (1 - c) * hr + i * qr, qr)
            send(piece, piece, c_send.at[slot, i], c_recv.at[slot, i], me, partner).wait_recv()

    def core_copies(buf, core, slot):
        hr, qr = core.shape[-2], core.shape[-2] // xs
        return [
            send(
                rows(buf, (1 - c) * hr + xi * qr, qr), rows(core, xi * qr, qr),
                c_send.at[slot, i], c_recv.at[slot, i], me, partner,
            )
            for i, xi in enumerate(order)
        ]

    def scatter_start(buf, core, slot):
        start(*core_copies(buf, core, slot))

    def scatter_pass(buf, core, halved, part, slot):
        hr, qr = core.shape[-2], core.shape[-2] // xs
        copies = core_copies(buf, core, slot)
        late = None
        for i, xi in enumerate(order):
            copies[i].wait_recv()
            mine = rows(buf, c * hr + xi * qr, qr)[...] + rows(core, xi * qr, qr)[...]
            if i < xs - 1:
                piece = rows(halved, xi * qr, qr)
                piece[...] = mine
                now = send(
                    piece, part.at[x], x_send.at[slot, i], x_recv.at[slot, x], me, xi * CORES + c
                )
            else:
                part[x] = mine
                now = None
            if late is not None:
                start(late)
            late = now

    def scatter_end(halved, part, slot):
        qr = halved.shape[-2] // xs
        for i in range(xs - 1):
            send(
                rows(halved, order[i] * qr, qr), part.at[order[i]],
                x_send.at[slot, i], x_recv.at[slot, order[i]], me, order[i] * CORES + c,
            ).wait_recv()
        total = part[0]
        for i in range(1, xs):
            total = total + part[i]
        return total

    def scalar_start(rnd, stage, value):
        sums[rnd, stage, places[stage]] = value
        own = sums.at[rnd, stage, places[stage]]
        for d, (peer, _) in enumerate(groups[stage]):
            start(send(own, own, s_send.at[rnd, stage, d], s_recv.at[rnd, stage, places[stage]], *peer))

    def scalar_wait(rnd, stage):
        for d, (peer, place) in enumerate(groups[stage]):
            slot = sums.at[rnd, stage, place]
            send(slot, slot, s_send.at[rnd, stage, d], s_recv.at[rnd, stage, place], *peer).wait_recv()
        total = sums[rnd, stage, 0]
        for i in range(1, len(groups[stage]) + 1):
            total = total + sums[rnd, stage, i]
        return total

    def tile_of(values):
        values = values + [jnp.zeros((8 - len(values), half), F32)]
        return jnp.concatenate(values, axis=0)

    prepare_both(0)
    for copy in loads:
        copy.wait()
    pl.semaphore_wait(barrier, len(greeted))
    psi_rows = width // tg
    psi_piece = rows(got_psi, c * half + x * psi_rows, psi_rows)
    psi_copy = send(
        rows(psi.at[2], c * half + x * psi_rows, psi_rows), psi_piece,
        one_send.at[0], one_recv.at[0], up, lane,
    )
    start(psi_copy)

    @pl.loop(1, terms)
    def _(t):
        prepare_both(t)
        for copy in ops_copies(t - 1):
            copy.start()

    rows_own = left_dims[me]
    rows_next = jnp.where(me + 1 < ns, left_dims[up], 0)
    cols_own = right_dims[me]
    cols_last = jnp.where(me >= 1, right_dims[down], 0)
    live_rows = [rows_own, rows_next, rows_next]
    live_cols = [cols_own, cols_own, cols_last]

    def mask_of(k, first_row, count):
        row = lax.broadcasted_iota(jnp.int32, (count, width), 0) + first_row
        col = lax.broadcasted_iota(jnp.int32, (count, width), 1)
        return (row < live_rows[k]) & (col < live_cols[k])

    for k in range(2):
        vec[k] = jnp.where(mask_of(k, 0, width), psi[k].astype(F32), 0.0).astype(BF16)
    for copy in ops_copies(terms - 1):
        copy.start()
    psi_copy.wait_recv()
    gather_start(got_psi, 4)

    def part_own(t, blocks, images, total):
        image = dot(sl0[t], blocks[0]).astype(BF16)
        images[t, 0] = image
        total[0] += dot(image, sr0[t])

    def part_near(t, blocks, images, total):
        one = dot(sl1[t], blocks[1]).astype(BF16)
        two = dot(sl1[t], blocks[2]).astype(BF16)
        images[t, 1] = one
        images[t, 2] = two
        total[1] += dot(one, sr0[t])
        total[2] += dot(two, sr1[t])

    scale, each = NOISE_WEIGHT / (terms * tg), 1.0 / tg

    def grow(out, one, two, t, blocks):
        for k in blocks:
            out[min(k, 1)] += dot_t(one[t, k], two[t, k])

    def put_folded(slot, group, full):
        mats[slot, group, :half] = full[:half, :half]
        mats[slot, group, half:width] = full[:half, half:]
        mats[slot, group, width:] = full[half:, half:]

    acc[...] = jnp.zeros_like(acc)
    n_one[...] = jnp.zeros_like(n_one)

    @pl.loop(0, terms)
    def _(t):
        part_own(t, vec, img_a, acc)

    gather_pass(got_psi, 4)

    @pl.loop(0, terms)
    def _(t):
        grow(n_one, img_a, img_a, t, (0,))

    gather_end(got_psi, 4)
    vec[2] = jnp.where(mask_of(2, 0, width), got_psi[...].astype(F32), 0.0).astype(BF16)

    @pl.loop(0, terms)
    def _(t):
        for copy in ops_copies(t):
            copy.wait_recv()
        restore(t, got_l, sl1)
        restore(t, got_r, sr1)
        part_near(t, vec, img_a, acc)

        @pl.when(t > 0)
        def _():
            grow(n_one, img_a, img_a, t - 1, (1, 2))

    scatter_start(acc, core_a, 0)
    h11 = a11 = jnp.zeros((1, half), F32)
    for k in range(3):
        wide = vec[k].astype(F32)
        h11 = h11 + fold(wide * acc[k])
        a11 = a11 + fold(wide * wide)
    scalar_start(0, 0, tile_of([h11, a11]))
    scatter_pass(acc, core_a, half_a, part_a, 0)
    grow(n_one, img_a, img_a, terms - 1, (1, 2))
    put_folded(0, 0, scale * n_one[0] + each * dot_t(vec[0], vec[0]))
    put_folded(0, 1, scale * n_one[1] + each * (dot_t(vec[1], vec[1]) + dot_t(vec[2], vec[2])))
    acc_b[...] = jnp.zeros_like(acc_b)
    total = jnp.sum(scalar_wait(0, 0), axis=1, keepdims=True)
    h_here, a_here = total[0:1], total[1:2] * (1.0 / tg)
    some = a_here > 0.0
    level = jnp.where(some, h_here / jnp.where(some, a_here, 1.0), 0.0)
    shard = scatter_end(half_a, part_a, 0)
    quarter = half // xs
    own_row = pl.multiple_of(c * half + x * quarter, quarter)
    for k in range(3):
        held = vec[k, pl.ds(own_row, quarter), :].astype(F32)
        inside_k = jnp.where(mask_of(k, own_row, quarter), shard[k], 0.0)
        cor[k, pl.ds(own_row, quarter), :] = (inside_k - level * held).astype(BF16)
    gather_start(cor, 5)
    gather_pass(cor, 5)
    gather_end(cor, 5)
    scatter_start(mats.at[0], core_m.at[0], 1)

    @pl.loop(0, terms)
    def _(t):
        part_own(t, cor, img_b, acc_b)
        part_near(t, cor, img_b, acc_b)

    vc = cc = vhc = chc = jnp.zeros((1, half), F32)
    for k in range(3):
        wide, corr = vec[k].astype(F32), cor[k].astype(F32)
        summed = acc_b[k]
        vc = vc + fold(wide * corr)
        cc = cc + fold(corr * corr)
        vhc = vhc + fold(wide * summed)
        chc = chc + fold(corr * summed)
    scalar_start(1, 0, tile_of([
        a11 * (1.0 / tg),
        h11,
        (vc + level * a11) * (1.0 / tg),
        (cc + level * (2.0 * vc + level * a11)) * (1.0 / tg),
        vhc + level * h11,
        chc + level * (2.0 * vhc + level * h11),
    ]))
    scatter_pass(mats.at[0], core_m.at[0], half_m.at[0], part_m.at[0], 1)
    n_one[...] = jnp.zeros_like(n_one)
    n_two[...] = jnp.zeros_like(n_two)

    @pl.loop(0, terms)
    def _(t):
        grow(n_one, img_b, img_b, t, (0, 1, 2))

    put_folded(1, 0, scale * n_one[0] + each * dot_t(cor[0], cor[0]))
    put_folded(1, 1, scale * n_one[1] + each * (dot_t(cor[1], cor[1]) + dot_t(cor[2], cor[2])))
    scatter_start(mats.at[1], core_m.at[1], 2)
    scalar_start(1, 1, scalar_wait(1, 0))

    @pl.loop(0, terms)
    def _(t):
        grow(n_two, img_a, img_b, t, (0, 1, 2))

    cross = scale * n_two[0] + each * dot_t(vec[0], cor[0])
    put_folded(2, 0, cross + cross.T)
    cross = scale * n_two[1] + each * (dot_t(vec[1], cor[1]) + dot_t(vec[2], cor[2]))
    put_folded(2, 1, cross + cross.T)
    scatter_start(mats.at[2], core_m.at[2], 3)
    scatter_pass(mats.at[1], core_m.at[1], half_m.at[1], part_m.at[1], 2)
    scatter_pass(mats.at[2], core_m.at[2], half_m.at[2], part_m.at[2], 3)
    scalar_start(1, 2, scalar_wait(1, 1))
    shares = [scatter_end(half_m.at[q], part_m.at[q], 1 + q) for q in range(3)]
    count = shares[0].shape[1]
    for q in range(3):
        hop_out[q * count:(q + 1) * count] = shares[q][1]
    hop_out[3 * count:] = jnp.broadcast_to(level, (8, half))
    hop = send(hop_out, hop_in, one_send.at[1], one_recv.at[1], up, lane)
    start(hop)
    whole = jnp.sum(scalar_wait(1, 2), axis=1, keepdims=True)
    a11, h11 = whole[0:1], whole[1:2]
    mean = h11 / a11
    a12 = whole[2:3] - mean * a11
    a22 = whole[3:4] - mean * (2.0 * whole[2:3] - mean * a11)
    h12 = whole[4:5] - mean * h11
    h22 = whole[5:6] - mean * (2.0 * whole[4:5] - mean * h11)
    quad_a = a11 * a22 - a12 * a12
    quad_b = h11 * a22 + h22 * a11 - 2.0 * h12 * a12
    quad_c = h11 * h22 - h12 * h12
    lowest = (quad_b - jnp.sqrt(jnp.maximum(quad_b * quad_b - 4.0 * quad_a * quad_c, 0.0))) / (
        2.0 * quad_a
    )
    ratio = (lowest * a11 - h11) / (h12 - lowest * a12)
    first_coef = lax.rsqrt(a11 + 2.0 * ratio * a12 + ratio * ratio * a22)
    second_coef = ratio * first_coef
    energy[...] = lowest

    def weigh(coef, parts):
        return coef * coef * parts[0] + coef * second_coef * parts[2] + second_coef * second_coef * parts[1]

    coef = first_coef + second_coef * (level - mean)
    stay = weigh(coef, [shares[q][0] for q in range(3)])
    hop.wait_recv()
    coef_last = first_coef + second_coef * (hop_in[3 * count:3 * count + 1, 0:1] - mean)
    come = weigh(coef_last, [hop_in[q * count:(q + 1) * count] for q in range(3)])
    rows(folded, (c * xs + x) * count, count)[...] = stay + come
    ns_two[...] = (coef * vec[2].astype(F32) + second_coef * cor[2].astype(F32)).astype(BF16)
    gather_start(folded, 6)
    for k in range(2):
        new_state[k] = (coef * vec[k].astype(F32) + second_coef * cor[k].astype(F32)).astype(BF16)
    ns_copy = send(ns_two, ns_got, one_send.at[2], one_recv.at[2], down, lane)
    start(ns_copy)
    gather_pass(folded, 6)
    gather_end(folded, 6)

    row = lax.broadcasted_iota(jnp.int32, (width, width), 0)
    col = lax.broadcasted_iota(jnp.int32, (width, width), 1)
    identity = jnp.where(row == col, 1.0, 0.0).astype(F32)
    corner = folded[half:width]
    density = jnp.concatenate([
        jnp.concatenate([folded[:half], corner], axis=1),
        jnp.concatenate([corner.T, folded[width:]], axis=1),
    ], axis=0)
    density = jnp.where((row < rows_own) & (col < rows_own), density, 0.0)
    trace = jnp.sum(jnp.sum(density * identity, axis=0, keepdims=True), axis=1, keepdims=True)
    live = jnp.broadcast_to(rows_own, (1, 1)).astype(F32)
    shifted = density - (trace / live) * identity
    square = jnp.sum(jnp.sum(shifted * shifted, axis=0, keepdims=True), axis=1, keepdims=True)
    kept[...] = shifted / jnp.sqrt(square)

    @pl.loop(0, SIGN_STEPS)
    def _(step):
        current = kept[...]
        parts = halves(current)
        squared = dot_wide(parts, parts)
        cubed = dot_wide(halves(squared), parts)
        kept[...] = 1.5 * current - 0.5 * cubed

    kept[...] = 0.5 * (identity + kept[...])

    ns_copy.wait_recv()
    new_state[2] = ns_got[...]

    @pl.loop(0, terms)
    def _(t):
        for copy in ops_copies(t):
            copy.wait_send()

    for copy in waits:
        copy.wait_send()


def per_device(zs, ns, tg, psi, left_ops, right_ops, left_dims, right_dims):
    terms, width = left_ops.shape[0], left_ops.shape[-1]
    half, xs = width // 2, tg // CORES
    quarter, ys = half // xs, ns // zs
    tall = 3 * half
    share = tall // 2 // xs
    most = max(tg, zs, ys)
    vmem, hbm = pl.BlockSpec(memory_space=pltpu.VMEM), pl.BlockSpec(memory_space=pltpu.HBM)
    dma = pltpu.SemaphoreType.DMA
    state, kept, energy = pl.pallas_call(
        functools.partial(kernel, (ns, zs, tg, terms, width)),
        out_shape=(
            jax.ShapeDtypeStruct((3, width, width), BF16),
            jax.ShapeDtypeStruct((width, width), F32),
            jax.ShapeDtypeStruct((1, 1), F32),
        ),
        in_specs=[hbm] * 5,
        out_specs=(vmem, vmem, vmem),
        scratch_shapes=[pltpu.SMEM((ns,), jnp.int32)] * 2
        + [pltpu.VMEM((3, width, width), BF16)]
        + [pltpu.VMEM((terms, width, width), BF16)] * 6
        + [pltpu.VMEM((terms, width + 16, half), BF16)] * 4
        + [pltpu.VMEM((width, width), BF16)]
        + [pltpu.VMEM((3, width, width), BF16)] * 2
        + [pltpu.VMEM((terms, 3, width, width), BF16)] * 2
        + [pltpu.VMEM((3, width, width), F32)] * 2
        + [pltpu.VMEM((3, half, width), F32)] * 2
        + [pltpu.VMEM((xs, 3, quarter, width), F32)]
        + [pltpu.VMEM((2, width, width), F32)] * 2
        + [pltpu.VMEM((3, 2, tall, half), F32)]
        + [pltpu.VMEM((3, 2, tall // 2, half), F32)] * 2
        + [pltpu.VMEM((3, xs, 2, share, half), F32)]
        + [pltpu.VMEM((3 * share + 8, half), F32)] * 2
        + [pltpu.VMEM((tall, half), F32)]
        + [pltpu.VMEM((2, 3, most, 8, half), F32)]
        + [pltpu.VMEM((width, width), BF16)] * 2
        + [dma((4, terms)), dma((2, terms)), dma((2, terms)), dma((3,)), dma((3,))]
        + [dma((7, xs))] * 4
        + [dma((2, 3, most))] * 2,
        compiler_params=pltpu.CompilerParams(
            collective_id=0, has_side_effects=True, vmem_limit_bytes=48 << 20
        ),
    )(left_dims, right_dims, psi[0], left_ops[:, 0], right_ops[:, 0])
    return state[None], kept[None], energy[0, 0]


def solution(mesh):
    ns, tg = mesh.shape["sec"], mesh.shape["term"]
    zs = ZSIZE if ns % ZSIZE == 0 and ns > ZSIZE else 2
    in_specs = (
        P("sec", None, None, None),
        P("term", "sec", None, None),
        P("term", "sec", None, None),
        P(),
        P(),
    )
    out_specs = (P("sec", None, None, None), P("sec", None, None), P())
    return jax.shard_map(
        functools.partial(per_device, zs, ns, tg),
        mesh=mesh, in_specs=in_specs, out_specs=out_specs, check_vma=False,
    )
```

```python
import functools

import jax
import jax.numpy as jnp
from jax import lax
from jax.experimental import pallas as pl
from jax.experimental.pallas import tpu as pltpu
from jax.sharding import PartitionSpec as P

SIGN_STEPS = 6
ZSIZE = 8
CORES = 2
NOISE_WEIGHT = 0.5
MESH = pl.DeviceIdType.MESH
F32 = jnp.float32
BF16 = jnp.bfloat16


def dot(a, b):
    return jnp.dot(a, b, preferred_element_type=F32)


def dot_t(a, b):
    return lax.dot_general(a, b, (((1,), (1,)), ((), ())), preferred_element_type=F32)


def halves(value):
    high = value.astype(BF16)
    return high, (value - high.astype(F32)).astype(BF16)


def dot_wide(a, b):
    (ah, al), (bh, bl) = a, b
    return dot(jnp.concatenate([ah, ah, al], axis=1), jnp.concatenate([bh, bl, bh], axis=0))


def fold(value):
    half = value.shape[1] // 2
    row = jnp.sum(value, axis=0, keepdims=True)
    return row[:, :half] + row[:, half:]


def kernel(
    sizes,
    left_dims_hbm, right_dims_hbm, psi_hbm, left_hbm, right_hbm,
    new_state, kept, energy,
    left_dims, right_dims, psi, left, right,
    sl0, sr0, sl1, sr1, pack_l, pack_r, got_l, got_r, got_psi,
    vec, cor, img_a, img_b, acc, acc_b, core_a, half_a, part_a, part_b,
    nacc, mats, core_m, half_m, part_m, part_n, hop_out, hop_in, folded,
    sums, ns_two, ns_got,
    in_sem, pack_send, pack_recv, one_send, one_recv, c_send, c_recv, x_send, x_recv, s_send, s_recv,
):
    ns, zs, tg, terms, width = sizes
    ys, xs = ns // zs, tg // CORES
    half = width // 2
    me, lane = lax.axis_index("sec"), lax.axis_index("term")
    x, c = lax.div(lane, CORES), lax.rem(lane, CORES)
    y, z = lax.div(me, zs), lax.rem(me, zs)
    up, down = lax.rem(me + 1, ns), lax.rem(me + ns - 1, ns)
    partner = lane + 1 - 2 * c
    far_first = sorted(range(1, xs), key=lambda d: -min(d, xs - d))
    order = [lax.rem(x + d, xs) for d in far_first] + [x]

    def send(src, dst, ssem, rsem, sec, term):
        return pltpu.make_async_remote_copy(
            src_ref=src, dst_ref=dst, send_sem=ssem, recv_sem=rsem,
            device_id=(sec, term), device_id_type=MESH,
        )

    barrier = pltpu.get_barrier_semaphore()
    groups = [
        [((me, lax.rem(lane + d, tg)), lax.rem(lane + d, tg)) for d in range(1, tg)],
        [((y * zs + lax.rem(z + d, zs), lane), lax.rem(z + d, zs)) for d in range(1, zs)],
        [((lax.rem(y + d, ys) * zs + z, lane), lax.rem(y + d, ys)) for d in range(1, ys)],
    ]
    places = [lane, z, y]
    greeted = [peer for group in groups for peer, _ in group] + [(up, lane), (down, lane)]
    for peer in greeted:
        pl.semaphore_signal(barrier, inc=1, device_id=peer, device_id_type=MESH)

    def load(src, dst, slot):
        return pltpu.make_async_copy(src, dst, in_sem.at[slot])

    rest = pl.ds(1, terms - 1)
    loads = [
        load(left_hbm.at[0], left.at[0], 0),
        load(right_hbm.at[0], right.at[0], 1),
        load(psi_hbm, psi, 2),
        load(left_hbm.at[rest], left.at[rest], 3),
        load(right_hbm.at[rest], right.at[rest], 4),
        load(left_dims_hbm, left_dims, 5),
        load(right_dims_hbm, right_dims, 6),
    ]
    for copy in loads:
        copy.start()

    row_h = lax.broadcasted_iota(jnp.int32, (half, half), 0)
    col_h = lax.broadcasted_iota(jnp.int32, (half, half), 1)

    def prepare(t, raw, sym, pack):
        wide = raw[t].astype(F32)
        whole = (wide + wide.T).astype(BF16)
        sym[t] = whole
        again = whole.astype(F32)
        low, high = again[:half, :half], again[half:, half:]
        pack[t, :half] = whole[:half, half:]
        pack[t, half:width] = jnp.where(row_h <= col_h, low, high).astype(BF16)
        diag = jnp.sum(jnp.where(row_h == col_h, high, 0.0), axis=0, keepdims=True)
        pack[t, width:] = jnp.broadcast_to(diag, (16, half)).astype(BF16)

    def restore(t, pack, sym):
        corner = pack[t, :half].astype(F32)
        mixed = pack[t, half:width].astype(F32)
        diag = pack[t, width:].astype(F32)[0:1]
        turned = mixed.T
        sym[t, :half, :half] = jnp.where(row_h <= col_h, mixed, turned).astype(BF16)
        sym[t, :half, half:] = pack[t, :half]
        sym[t, half:, :half] = corner.T.astype(BF16)
        lower = jnp.where(row_h == col_h, jnp.broadcast_to(diag, (half, half)), turned)
        sym[t, half:, half:] = jnp.where(row_h > col_h, mixed, lower).astype(BF16)

    def ops_copies(t):
        return (
            send(pack_l.at[t], got_l.at[t], pack_send.at[0, t], pack_recv.at[0, t], down, lane),
            send(pack_r.at[t], got_r.at[t], pack_send.at[1, t], pack_recv.at[1, t], up, lane),
        )

    def prepare_both(t):
        prepare(t, left, sl0, pack_l)
        prepare(t, right, sr0, pack_r)

    waits = []

    def start(*copies):
        for copy in copies:
            copy.start()
        waits.extend(copies)

    def rows(ref, first, count):
        return ref.at[..., pl.ds(pl.multiple_of(first, count), count), :]

    def gather_start(ref, slot):
        hr, qr = ref.shape[-2] // 2, ref.shape[-2] // 2 // xs
        own = rows(ref, c * hr + x * qr, qr)
        for i, d in enumerate(far_first):
            start(send(own, own, x_send.at[slot, i], x_recv.at[slot, x], me, order[i] * CORES + c))
        start(send(own, own, c_send.at[slot, x], c_recv.at[slot, x], me, partner))

    def gather_pass(ref, slot):
        hr, qr = ref.shape[-2] // 2, ref.shape[-2] // 2 // xs
        for i in reversed(range(len(far_first))):
            piece = rows(ref, c * hr + order[i] * qr, qr)
            send(
                piece, piece, x_send.at[slot, i], x_recv.at[slot, order[i]], me, order[i] * CORES + c
            ).wait_recv()
            start(send(piece, piece, c_send.at[slot, order[i]], c_recv.at[slot, order[i]], me, partner))

    def gather_end(ref, slot):
        hr, qr = ref.shape[-2] // 2, ref.shape[-2] // 2 // xs
        for i in range(xs):
            piece = rows(ref, (1 - c) * hr + i * qr, qr)
            send(piece, piece, c_send.at[slot, i], c_recv.at[slot, i], me, partner).wait_recv()

    def core_copies(buf, core, slot):
        hr, qr = core.shape[-2], core.shape[-2] // xs
        return [
            send(
                rows(buf, (1 - c) * hr + xi * qr, qr), rows(core, xi * qr, qr),
                c_send.at[slot, i], c_recv.at[slot, i], me, partner,
            )
            for i, xi in enumerate(order)
        ]

    def scatter_start(buf, core, slot):
        start(*core_copies(buf, core, slot))

    def scatter_pass(buf, core, halved, part, slot):
        hr, qr = core.shape[-2], core.shape[-2] // xs
        copies = core_copies(buf, core, slot)
        late = None
        for i, xi in enumerate(order):
            copies[i].wait_recv()
            mine = rows(buf, c * hr + xi * qr, qr)[...] + rows(core, xi * qr, qr)[...]
            if i < xs - 1:
                piece = rows(halved, xi * qr, qr)
                piece[...] = mine
                now = send(
                    piece, part.at[x], x_send.at[slot, i], x_recv.at[slot, x], me, xi * CORES + c
                )
            else:
                part[x] = mine
                now = None
            if late is not None:
                start(late)
            late = now

    def scatter_end(halved, part, slot):
        qr = halved.shape[-2] // xs
        for i in range(xs - 1):
            send(
                rows(halved, order[i] * qr, qr), part.at[order[i]],
                x_send.at[slot, i], x_recv.at[slot, order[i]], me, order[i] * CORES + c,
            ).wait_recv()
        total = part[0]
        for i in range(1, xs):
            total = total + part[i]
        return total

    def scalar_start(rnd, stage, value):
        sums[rnd, stage, places[stage]] = value
        own = sums.at[rnd, stage, places[stage]]
        for d, (peer, _) in enumerate(groups[stage]):
            start(send(own, own, s_send.at[rnd, stage, d], s_recv.at[rnd, stage, places[stage]], *peer))

    def scalar_wait(rnd, stage):
        for d, (peer, place) in enumerate(groups[stage]):
            slot = sums.at[rnd, stage, place]
            send(slot, slot, s_send.at[rnd, stage, d], s_recv.at[rnd, stage, place], *peer).wait_recv()
        total = sums[rnd, stage, 0]
        for i in range(1, len(groups[stage]) + 1):
            total = total + sums[rnd, stage, i]
        return total

    def tile_of(values):
        values = values + [jnp.zeros((8 - len(values), half), F32)]
        return jnp.concatenate(values, axis=0)

    loads[0].wait()
    loads[1].wait()
    prepare_both(0)
    loads[2].wait()
    pl.semaphore_wait(barrier, len(greeted))
    psi_rows = width // tg
    psi_piece = rows(got_psi, c * half + x * psi_rows, psi_rows)
    psi_copy = send(
        rows(psi.at[2], c * half + x * psi_rows, psi_rows), psi_piece,
        one_send.at[0], one_recv.at[0], up, lane,
    )
    start(psi_copy)
    for copy in loads[3:]:
        copy.wait()

    @pl.loop(1, terms)
    def _(t):
        prepare_both(t)
        for copy in ops_copies(t - 1):
            copy.start()

    rows_own = left_dims[me]
    rows_next = jnp.where(me + 1 < ns, left_dims[up], 0)
    cols_own = right_dims[me]
    cols_last = jnp.where(me >= 1, right_dims[down], 0)
    live_rows = [rows_own, rows_next, rows_next]
    live_cols = [cols_own, cols_own, cols_last]

    def mask_of(k, first_row, count):
        row = lax.broadcasted_iota(jnp.int32, (count, width), 0) + first_row
        col = lax.broadcasted_iota(jnp.int32, (count, width), 1)
        return (row < live_rows[k]) & (col < live_cols[k])

    for k in range(2):
        vec[k] = jnp.where(mask_of(k, 0, width), psi[k].astype(F32), 0.0).astype(BF16)
    for copy in ops_copies(terms - 1):
        copy.start()

    scale, each = NOISE_WEIGHT / (terms * tg), 1.0 / tg
    quarter = half // xs
    own_row = pl.multiple_of(c * half + x * quarter, quarter)
    teams = [(0,), (1, 2)]

    def part_own(t, blocks, images, total):
        image = dot(sl0[t], blocks[0]).astype(BF16)
        images[t, 0] = image
        total[0] += dot(image, sr0[t])

    def part_one(t, blocks, images, total):
        image = dot(sl1[t], blocks[1]).astype(BF16)
        images[t, 1] = image
        total[1] += dot(image, sr0[t])

    def part_two(t, blocks, images, total):
        image = dot(sl1[t], blocks[2]).astype(BF16)
        images[t, 2] = image
        total[2] += dot(image, sr1[t])

    def grow(slot, team, one, two, t):
        for k in teams[team]:
            nacc[team, slot] += dot_t(one[t, k], two[t, k])

    def put_folded(slot, team, full):
        mats[team, slot, :half] = full[:half, :half]
        mats[team, slot, half:width] = full[:half, half:]
        mats[team, slot, width:] = full[half:, half:]

    def own_part(team, one, two):
        total = dot_t(one[teams[team][0]], two[teams[team][0]])
        for k in teams[team][1:]:
            total = total + dot_t(one[k], two[k])
        return each * total

    def put_plain(slot, team, one):
        put_folded(slot, team, scale * nacc[team, slot] + own_part(team, one, one))

    def put_cross(slot, team, one, two):
        cross = scale * nacc[team, slot] + own_part(team, one, two)
        put_folded(slot, team, cross + cross.T)

    def norms(team):
        h_row = a_row = jnp.zeros((1, half), F32)
        for k in teams[team]:
            wide = vec[k].astype(F32)
            h_row = h_row + fold(wide * acc[k])
            a_row = a_row + fold(wide * wide)
        return h_row, a_row

    def level_of(rnd):
        total = jnp.sum(scalar_wait(rnd, 0), axis=1, keepdims=True)
        h_here, a_here = total[0:1], total[1:2] * each
        some = a_here > 0.0
        return jnp.where(some, h_here / jnp.where(some, a_here, 1.0), 0.0)

    def correct(team, level, shard):
        for i, k in enumerate(teams[team]):
            held = vec[k, pl.ds(own_row, quarter), :].astype(F32)
            inside_k = jnp.where(mask_of(k, own_row, quarter), shard[i], 0.0)
            cor[k, pl.ds(own_row, quarter), :] = (inside_k - level * held).astype(BF16)

    near = pl.ds(1, 2)
    acc_of = [acc.at[pl.ds(0, 1)], acc.at[near]]
    core_of = [core_a.at[pl.ds(0, 1)], core_a.at[near]]
    half_of = [half_a.at[pl.ds(0, 1)], half_a.at[near]]
    part_of = [part_a, part_b]
    cor_of = [cor.at[pl.ds(0, 1)], cor.at[near]]

    def arrive(t):
        for copy in ops_copies(t):
            copy.wait_recv()
        restore(t, got_l, sl1)
        restore(t, got_r, sr1)

    acc[...] = jnp.zeros_like(acc)
    acc_b[...] = jnp.zeros_like(acc_b)
    nacc[...] = jnp.zeros_like(nacc)

    @pl.loop(0, terms, unroll=True)
    def _(t):
        part_own(t, vec, img_a, acc)

    scatter_start(acc_of[0], core_of[0], 0)
    h_zero, a_zero = norms(0)
    scalar_start(0, 0, tile_of([h_zero, a_zero]))
    psi_copy.wait_recv()
    gather_start(got_psi, 8)
    scatter_pass(acc_of[0], core_of[0], half_of[0], part_of[0], 0)

    @pl.loop(0, terms, unroll=True)
    def _(t):
        grow(0, 0, img_a, img_a, t)

    early = terms // 4
    for t in range(early):
        arrive(t)
        part_one(t, vec, img_a, acc)
    gather_pass(got_psi, 8)
    level_zero = level_of(0)
    shard = scatter_end(half_of[0], part_of[0], 0)
    correct(0, level_zero, shard)
    gather_start(cor_of[0], 9)
    gather_end(got_psi, 8)
    vec[2] = jnp.where(mask_of(2, 0, width), got_psi[...].astype(F32), 0.0).astype(BF16)
    for t in range(early):
        part_two(t, vec, img_a, acc)
    middle = terms // 2
    for t in range(early, middle):
        arrive(t)
        part_one(t, vec, img_a, acc)
        part_two(t, vec, img_a, acc)
    gather_pass(cor_of[0], 9)
    for t in range(middle, middle + 1):
        arrive(t)
        part_one(t, vec, img_a, acc)
        part_two(t, vec, img_a, acc)
    gather_end(cor_of[0], 9)

    @pl.loop(0, terms, unroll=True)
    def _(t):
        part_own(t, cor, img_b, acc_b)

    for t in range(middle + 1, terms):
        arrive(t)
        part_one(t, vec, img_a, acc)
        part_two(t, vec, img_a, acc)
    scatter_start(acc_of[1], core_of[1], 1)
    h_near, a_near = norms(1)
    scalar_start(1, 0, tile_of([h_near, a_near]))

    @pl.loop(0, terms, unroll=True)
    def _(t):
        grow(1, 0, img_b, img_b, t)

    scatter_pass(acc_of[1], core_of[1], half_of[1], part_of[1], 1)

    @pl.loop(0, terms, unroll=True)
    def _(t):
        grow(2, 0, img_a, img_b, t)

    put_plain(0, 0, vec)
    put_plain(1, 0, cor)
    put_cross(2, 0, vec, cor)
    scatter_start(mats.at[0], core_m.at[0], 2)
    level_near = level_of(1)
    shard = scatter_end(half_of[1], part_of[1], 1)
    correct(1, level_near, shard)
    gather_start(cor_of[1], 10)

    @pl.loop(0, terms, unroll=True)
    def _(t):
        grow(0, 1, img_a, img_a, t)

    put_plain(0, 1, vec)
    scatter_start(mats.at[1, 0], core_m.at[1, 0], 3)
    gather_pass(cor_of[1], 10)
    gather_end(cor_of[1], 10)

    scatter_pass(mats.at[0], core_m.at[0], half_m.at[0], part_m, 2)

    @pl.loop(0, terms, unroll=True)
    def _(t):
        part_one(t, cor, img_b, acc_b)
        part_two(t, cor, img_b, acc_b)

    levels = [level_zero, level_near]
    sides = [(h_zero, a_zero), (h_near, a_near)]
    tile = 0.0
    for team in range(2):
        level, (h_row, a_row) = levels[team], sides[team]
        vc = cc = vhc = chc = jnp.zeros((1, half), F32)
        for k in teams[team]:
            wide, corr = vec[k].astype(F32), cor[k].astype(F32)
            summed = acc_b[k]
            vc = vc + fold(wide * corr)
            cc = cc + fold(corr * corr)
            vhc = vhc + fold(wide * summed)
            chc = chc + fold(corr * summed)
        tile = tile + tile_of([
            a_row * each,
            h_row,
            (vc + level * a_row) * each,
            (cc + level * (2.0 * vc + level * a_row)) * each,
            vhc + level * h_row,
            chc + level * (2.0 * vhc + level * h_row),
        ])
    scalar_start(2, 0, tile)
    scatter_pass(mats.at[1, 0], core_m.at[1, 0], half_m.at[1, 0], part_n.at[0], 3)

    @pl.loop(0, terms, unroll=True)
    def _(t):
        grow(1, 1, img_b, img_b, t)

    put_plain(1, 1, cor)
    scatter_start(mats.at[1, 1], core_m.at[1, 1], 4)

    @pl.loop(0, terms, unroll=True)
    def _(t):
        grow(2, 1, img_a, img_b, t)

    put_cross(2, 1, vec, cor)
    scatter_start(mats.at[1, 2], core_m.at[1, 2], 5)
    scatter_pass(mats.at[1, 1], core_m.at[1, 1], half_m.at[1, 1], part_n.at[1], 4)
    scalar_start(2, 1, scalar_wait(2, 0))
    scatter_pass(mats.at[1, 2], core_m.at[1, 2], half_m.at[1, 2], part_n.at[2], 5)
    stay = scatter_end(half_m.at[0], part_m, 2)
    count = stay.shape[1]
    for q in range(3):
        hop_out[q * count:(q + 1) * count] = scatter_end(half_m.at[1, q], part_n.at[q], 3 + q)
    hop_out[3 * count:] = jnp.broadcast_to(level_near, (8, half))
    hop = send(hop_out, hop_in, one_send.at[1], one_recv.at[1], up, lane)
    start(hop)
    scalar_start(2, 2, scalar_wait(2, 1))
    whole = jnp.sum(scalar_wait(2, 2), axis=1, keepdims=True)
    a11, h11 = whole[0:1], whole[1:2]
    mean = h11 / a11
    a12 = whole[2:3] - mean * a11
    a22 = whole[3:4] - mean * (2.0 * whole[2:3] - mean * a11)
    h12 = whole[4:5] - mean * h11
    h22 = whole[5:6] - mean * (2.0 * whole[4:5] - mean * h11)
    quad_a = a11 * a22 - a12 * a12
    quad_b = h11 * a22 + h22 * a11 - 2.0 * h12 * a12
    quad_c = h11 * h22 - h12 * h12
    lowest = (quad_b - jnp.sqrt(jnp.maximum(quad_b * quad_b - 4.0 * quad_a * quad_c, 0.0))) / (
        2.0 * quad_a
    )
    ratio = (lowest * a11 - h11) / (h12 - lowest * a12)
    first_coef = lax.rsqrt(a11 + 2.0 * ratio * a12 + ratio * ratio * a22)
    second_coef = ratio * first_coef
    energy[...] = lowest

    def weigh(coef, parts):
        return coef * coef * parts[0] + coef * second_coef * parts[2] + second_coef * second_coef * parts[1]

    coefs = [first_coef + second_coef * (level - mean) for level in levels]
    stay = weigh(coefs[0], [stay[q] for q in range(3)])
    hop.wait_recv()
    coef_last = first_coef + second_coef * (hop_in[3 * count:3 * count + 1, 0:1] - mean)
    come = weigh(coef_last, [hop_in[q * count:(q + 1) * count] for q in range(3)])
    rows(folded, (c * xs + x) * count, count)[...] = stay + come
    ns_two[...] = (coefs[1] * vec[2].astype(F32) + second_coef * cor[2].astype(F32)).astype(BF16)
    gather_start(folded, 11)
    for k in range(2):
        new_state[k] = (coefs[k] * vec[k].astype(F32) + second_coef * cor[k].astype(F32)).astype(BF16)
    ns_copy = send(ns_two, ns_got, one_send.at[2], one_recv.at[2], down, lane)
    start(ns_copy)
    gather_pass(folded, 11)
    gather_end(folded, 11)

    row = lax.broadcasted_iota(jnp.int32, (width, width), 0)
    col = lax.broadcasted_iota(jnp.int32, (width, width), 1)
    identity = jnp.where(row == col, 1.0, 0.0).astype(F32)
    corner = folded[half:width]
    density = jnp.concatenate([
        jnp.concatenate([folded[:half], corner], axis=1),
        jnp.concatenate([corner.T, folded[width:]], axis=1),
    ], axis=0)
    density = jnp.where((row < rows_own) & (col < rows_own), density, 0.0)
    trace = jnp.sum(jnp.sum(density * identity, axis=0, keepdims=True), axis=1, keepdims=True)
    live = jnp.broadcast_to(rows_own, (1, 1)).astype(F32)
    shifted = density - (trace / live) * identity
    square = jnp.sum(jnp.sum(shifted * shifted, axis=0, keepdims=True), axis=1, keepdims=True)
    kept[...] = shifted / jnp.sqrt(square)

    @pl.loop(0, SIGN_STEPS)
    def _(step):
        current = kept[...]
        parts = halves(current)
        squared = dot_wide(parts, parts)
        cubed = dot_wide(halves(squared), parts)
        kept[...] = 1.5 * current - 0.5 * cubed

    kept[...] = 0.5 * (identity + kept[...])

    ns_copy.wait_recv()
    new_state[2] = ns_got[...]

    @pl.loop(0, terms)
    def _(t):
        for copy in ops_copies(t):
            copy.wait_send()

    for copy in waits:
        copy.wait_send()


def per_device(zs, ns, tg, psi, left_ops, right_ops, left_dims, right_dims):
    terms, width = left_ops.shape[0], left_ops.shape[-1]
    half, xs = width // 2, tg // CORES
    quarter, ys = half // xs, ns // zs
    tall = 3 * half
    share = tall // 2 // xs
    most = max(tg, zs, ys)
    vmem, hbm = pl.BlockSpec(memory_space=pltpu.VMEM), pl.BlockSpec(memory_space=pltpu.HBM)
    dma = pltpu.SemaphoreType.DMA
    state, kept, energy = pl.pallas_call(
        functools.partial(kernel, (ns, zs, tg, terms, width)),
        out_shape=(
            jax.ShapeDtypeStruct((3, width, width), BF16),
            jax.ShapeDtypeStruct((width, width), F32),
            jax.ShapeDtypeStruct((1, 1), F32),
        ),
        in_specs=[hbm] * 5,
        out_specs=(vmem, vmem, vmem),
        scratch_shapes=[pltpu.SMEM((ns,), jnp.int32)] * 2
        + [pltpu.VMEM((3, width, width), BF16)]
        + [pltpu.VMEM((terms, width, width), BF16)] * 6
        + [pltpu.VMEM((terms, width + 16, half), BF16)] * 4
        + [pltpu.VMEM((width, width), BF16)]
        + [pltpu.VMEM((3, width, width), BF16)] * 2
        + [pltpu.VMEM((terms, 3, width, width), BF16)] * 2
        + [pltpu.VMEM((3, width, width), F32)] * 2
        + [pltpu.VMEM((3, half, width), F32)] * 2
        + [pltpu.VMEM((xs, 1, quarter, width), F32)]
        + [pltpu.VMEM((xs, 2, quarter, width), F32)]
        + [pltpu.VMEM((2, 3, width, width), F32)]
        + [pltpu.VMEM((2, 3, tall, half), F32)]
        + [pltpu.VMEM((2, 3, tall // 2, half), F32)] * 2
        + [pltpu.VMEM((xs, 3, share, half), F32)]
        + [pltpu.VMEM((3, xs, share, half), F32)]
        + [pltpu.VMEM((3 * share + 8, half), F32)] * 2
        + [pltpu.VMEM((tall, half), F32)]
        + [pltpu.VMEM((3, 3, most, 8, half), F32)]
        + [pltpu.VMEM((width, width), BF16)] * 2
        + [dma((7,)), dma((2, terms)), dma((2, terms)), dma((3,)), dma((3,))]
        + [dma((12, xs))] * 4
        + [dma((3, 3, most))] * 2,
        compiler_params=pltpu.CompilerParams(
            collective_id=0, has_side_effects=True, vmem_limit_bytes=67043328
        ),
    )(left_dims, right_dims, psi[0], left_ops[:, 0], right_ops[:, 0])
    return state[None], kept[None], energy[0, 0]


def solution(mesh):
    ns, tg = mesh.shape["sec"], mesh.shape["term"]
    zs = ZSIZE if ns % ZSIZE == 0 and ns > ZSIZE else 2
    in_specs = (
        P("sec", None, None, None),
        P("term", "sec", None, None),
        P("term", "sec", None, None),
        P(),
        P(),
    )
    out_specs = (P("sec", None, None, None), P("sec", None, None), P())
    return jax.shard_map(
        functools.partial(per_device, zs, ns, tg),
        mesh=mesh, in_specs=in_specs, out_specs=out_specs, check_vma=False,
    )
```

```python
import functools

import jax
import jax.numpy as jnp
from jax import lax
from jax.experimental import pallas as pl
from jax.experimental.pallas import tpu as pltpu
from jax.sharding import PartitionSpec as P

SIGN_STEPS = 6
ZSIZE = 8
CORES = 2
NOISE_WEIGHT = 0.5
MESH = pl.DeviceIdType.MESH
F32 = jnp.float32
BF16 = jnp.bfloat16


def dot(a, b):
    return jnp.dot(a, b, preferred_element_type=F32)


def dot_t(a, b):
    return lax.dot_general(a, b, (((1,), (1,)), ((), ())), preferred_element_type=F32)


def halves(value):
    high = value.astype(BF16)
    return high, (value - high.astype(F32)).astype(BF16)


def dot_wide(a, b):
    (ah, al), (bh, bl) = a, b
    return dot(jnp.concatenate([ah, ah, al], axis=1), jnp.concatenate([bh, bl, bh], axis=0))


def fold(value):
    half = value.shape[1] // 2
    row = jnp.sum(value, axis=0, keepdims=True)
    return row[:, :half] + row[:, half:]


def kernel(
    sizes,
    left_dims_hbm, right_dims_hbm, psi_hbm, left_hbm, right_hbm,
    state_hbm, folded_hbm,
    left_dims, right_dims, psi, left, right,
    sl0, sr0, sl1, sr1, pack_l, pack_r, got_l, got_r, got_psi,
    vec, cor, img_a, img_b, acc, acc_b, core_a, half_a, part_a,
    nacc, mats, core_m, half_m, part_m, part_n, hop_out, hop_in, folded,
    sums, ns_mine, cor_got, tag_out, tag_in,
    in_sem, pack_send, pack_recv, one_send, one_recv, c_send, c_recv, x_send, x_recv, s_send, s_recv,
):
    ns, zs, tg, terms, width = sizes
    ys, xs = ns // zs, tg // CORES
    half = width // 2
    me, lane = lax.axis_index("sec"), lax.axis_index("term")
    x, c = lax.div(lane, CORES), lax.rem(lane, CORES)
    y, z = lax.div(me, zs), lax.rem(me, zs)
    up, down = lax.rem(me + 1, ns), lax.rem(me + ns - 1, ns)
    partner = lane + 1 - 2 * c
    far_first = sorted(range(1, xs), key=lambda d: -min(d, xs - d))
    order = [lax.rem(x + d, xs) for d in far_first] + [x]

    def send(src, dst, ssem, rsem, sec, term):
        return pltpu.make_async_remote_copy(
            src_ref=src, dst_ref=dst, send_sem=ssem, recv_sem=rsem,
            device_id=(sec, term), device_id_type=MESH,
        )

    barrier = pltpu.get_barrier_semaphore()
    groups = [
        [((me, lax.rem(lane + d, tg)), lax.rem(lane + d, tg)) for d in range(1, tg)],
        [((y * zs + lax.rem(z + d, zs), lane), lax.rem(z + d, zs)) for d in range(1, zs)],
        [((lax.rem(y + d, ys) * zs + z, lane), lax.rem(y + d, ys)) for d in range(1, ys)],
    ]
    places = [lane, z, y]
    greeted = [peer for group in groups for peer, _ in group] + [(up, lane), (down, lane)]
    for peer in greeted:
        pl.semaphore_signal(barrier, inc=1, device_id=peer, device_id_type=MESH)

    def load(src, dst, slot):
        return pltpu.make_async_copy(src, dst, in_sem.at[slot])

    rest = pl.ds(1, terms - 1)
    loads = [
        load(left_hbm.at[0], left.at[0], 0),
        load(right_hbm.at[0], right.at[0], 1),
        load(psi_hbm, psi, 2),
        load(left_hbm.at[rest], left.at[rest], 3),
        load(right_hbm.at[rest], right.at[rest], 4),
        load(left_dims_hbm, left_dims, 5),
        load(right_dims_hbm, right_dims, 6),
    ]
    for copy in loads:
        copy.start()

    row_h = lax.broadcasted_iota(jnp.int32, (half, half), 0)
    col_h = lax.broadcasted_iota(jnp.int32, (half, half), 1)

    def prepare(t, raw, sym, pack):
        wide = raw[t].astype(F32)
        whole = (wide + wide.T).astype(BF16)
        sym[t] = whole
        again = whole.astype(F32)
        low, high = again[:half, :half], again[half:, half:]
        pack[t, :half] = whole[:half, half:]
        pack[t, half:width] = jnp.where(row_h <= col_h, low, high).astype(BF16)
        diag = jnp.sum(jnp.where(row_h == col_h, high, 0.0), axis=0, keepdims=True)
        pack[t, width:] = jnp.broadcast_to(diag, (8, half)).astype(BF16)

    def restore(t, pack, sym):
        corner = pack[t, :half].astype(F32)
        mixed = pack[t, half:width].astype(F32)
        diag = pack[t, width:].astype(F32)[0:1]
        turned = mixed.T
        sym[t, :half, :half] = jnp.where(row_h <= col_h, mixed, turned).astype(BF16)
        sym[t, :half, half:] = pack[t, :half]
        sym[t, half:, :half] = corner.T.astype(BF16)
        lower = jnp.where(row_h == col_h, jnp.broadcast_to(diag, (half, half)), turned)
        sym[t, half:, half:] = jnp.where(row_h > col_h, mixed, lower).astype(BF16)

    def ops_copies(t):
        return (
            send(pack_l.at[t], got_l.at[t], pack_send.at[0, t], pack_recv.at[0, t], down, lane),
            send(pack_r.at[t], got_r.at[t], pack_send.at[1, t], pack_recv.at[1, t], up, lane),
        )

    def prepare_both(t):
        prepare(t, left, sl0, pack_l)
        prepare(t, right, sr0, pack_r)

    waits = []

    def start(*copies):
        for copy in copies:
            copy.start()
        waits.extend(copies)

    def rows(ref, first, count):
        return ref.at[..., pl.ds(pl.multiple_of(first, count), count), :]

    def gather_start(ref, slot):
        hr, qr = ref.shape[-2] // 2, ref.shape[-2] // 2 // xs
        own = rows(ref, c * hr + x * qr, qr)
        for i, d in enumerate(far_first):
            start(send(own, own, x_send.at[slot, i], x_recv.at[slot, x], me, order[i] * CORES + c))
        start(send(own, own, c_send.at[slot, x], c_recv.at[slot, x], me, partner))

    def gather_pass(ref, slot):
        hr, qr = ref.shape[-2] // 2, ref.shape[-2] // 2 // xs
        for i in reversed(range(len(far_first))):
            piece = rows(ref, c * hr + order[i] * qr, qr)
            send(
                piece, piece, x_send.at[slot, i], x_recv.at[slot, order[i]], me, order[i] * CORES + c
            ).wait_recv()
            start(send(piece, piece, c_send.at[slot, order[i]], c_recv.at[slot, order[i]], me, partner))

    def gather_end(ref, slot):
        hr, qr = ref.shape[-2] // 2, ref.shape[-2] // 2 // xs
        for i in range(xs):
            piece = rows(ref, (1 - c) * hr + i * qr, qr)
            send(piece, piece, c_send.at[slot, i], c_recv.at[slot, i], me, partner).wait_recv()

    def core_copies(buf, core, slot):
        hr, qr = core.shape[-2], core.shape[-2] // xs
        return [
            send(
                rows(buf, (1 - c) * hr + xi * qr, qr), rows(core, xi * qr, qr),
                c_send.at[slot, i], c_recv.at[slot, i], me, partner,
            )
            for i, xi in enumerate(order)
        ]

    def scatter_start(buf, core, slot):
        start(*core_copies(buf, core, slot))

    def scatter_pass(buf, core, halved, part, slot):
        hr, qr = core.shape[-2], core.shape[-2] // xs
        copies = core_copies(buf, core, slot)
        late = None
        for i, xi in enumerate(order):
            copies[i].wait_recv()
            mine = rows(buf, c * hr + xi * qr, qr)[...] + rows(core, xi * qr, qr)[...]
            if i < xs - 1:
                piece = rows(halved, xi * qr, qr)
                piece[...] = mine
                now = send(
                    piece, part.at[x], x_send.at[slot, i], x_recv.at[slot, x], me, xi * CORES + c
                )
            else:
                part[x] = mine
                now = None
            if late is not None:
                start(late)
            late = now

    def scatter_end(halved, part, slot):
        qr = halved.shape[-2] // xs
        for i in range(xs - 1):
            send(
                rows(halved, order[i] * qr, qr), part.at[order[i]],
                x_send.at[slot, i], x_recv.at[slot, order[i]], me, order[i] * CORES + c,
            ).wait_recv()
        total = part[0]
        for i in range(1, xs):
            total = total + part[i]
        return total

    def scalar_start(rnd, stage, value):
        sums[rnd, stage, places[stage]] = value
        own = sums.at[rnd, stage, places[stage]]
        for d, (peer, _) in enumerate(groups[stage]):
            start(send(own, own, s_send.at[rnd, stage, d], s_recv.at[rnd, stage, places[stage]], *peer))

    def scalar_wait(rnd, stage):
        for d, (peer, place) in enumerate(groups[stage]):
            slot = sums.at[rnd, stage, place]
            send(slot, slot, s_send.at[rnd, stage, d], s_recv.at[rnd, stage, place], *peer).wait_recv()
        total = sums[rnd, stage, 0]
        for i in range(1, len(groups[stage]) + 1):
            total = total + sums[rnd, stage, i]
        return total

    one_hot = lax.broadcasted_iota(jnp.int32, (8, half), 0) == lax.broadcasted_iota(jnp.int32, (8, half), 1)

    def row_of(values):
        values = jnp.concatenate(values + [jnp.zeros((8 - len(values), half), F32)], axis=0)
        full = jnp.broadcast_to(jnp.sum(values, axis=1, keepdims=True), (8, half))
        return jnp.sum(jnp.where(one_hot, full, 0.0), axis=0, keepdims=True)

    def column_of(row):
        return jnp.sum(jnp.where(one_hot, jnp.broadcast_to(row, (8, half)), 0.0), axis=1, keepdims=True)

    loads[0].wait()
    loads[1].wait()
    prepare_both(0)
    loads[2].wait()
    pl.semaphore_wait(barrier, len(greeted))
    psi_rows = width // tg
    psi_piece = rows(got_psi, c * half + x * psi_rows, psi_rows)
    psi_copy = send(
        rows(psi.at[2], c * half + x * psi_rows, psi_rows), psi_piece,
        one_send.at[0], one_recv.at[0], up, lane,
    )
    start(psi_copy)
    for copy in loads[3:]:
        copy.wait()

    @pl.loop(1, terms)
    def _(t):
        prepare_both(t)
        for copy in ops_copies(t - 1):
            copy.start()

    rows_own = left_dims[me]
    rows_next = jnp.where(me + 1 < ns, left_dims[up], 0)
    cols_own = right_dims[me]
    cols_last = jnp.where(me >= 1, right_dims[down], 0)
    live_rows = [rows_own, rows_next, rows_next]
    live_cols = [cols_own, cols_own, cols_last]

    def mask_of(k, first_row, count):
        row = lax.broadcasted_iota(jnp.int32, (count, width), 0) + first_row
        col = lax.broadcasted_iota(jnp.int32, (count, width), 1)
        return (row < live_rows[k]) & (col < live_cols[k])

    for k in range(2):
        vec[k] = jnp.where(mask_of(k, 0, width), psi[k].astype(F32), 0.0).astype(BF16)
    for copy in ops_copies(terms - 1):
        copy.start()

    scale, each = NOISE_WEIGHT / (terms * tg), 1.0 / tg
    quarter = half // xs
    own_row = pl.multiple_of(c * half + x * quarter, quarter)
    teams = [(0,), (1, 2)]

    def part_own(t, blocks, images, total):
        image = dot(sl0[t], blocks[0]).astype(BF16)
        images[t, 0] = image
        total[0] += dot(image, sr0[t])

    def part_one(t, blocks, images, total):
        image = dot(sl1[t], blocks[1]).astype(BF16)
        images[t, 1] = image
        total[1] += dot(image, sr0[t])

    def part_two(t, blocks, images, total):
        image = dot(sl1[t], blocks[2]).astype(BF16)
        images[t, 2] = image
        total[2] += dot(image, sr1[t])

    def grow(slot, team, one, two, t):
        for k in teams[team]:
            nacc[team, slot] += dot_t(one[t, k], two[t, k])

    def put_folded(slot, team, full):
        mats[team, slot, :half] = full[:half, :half]
        mats[team, slot, half:width] = full[:half, half:]
        mats[team, slot, width:] = full[half:, half:]

    def own_part(team, one, two):
        total = dot_t(one[teams[team][0]], two[teams[team][0]])
        for k in teams[team][1:]:
            total = total + dot_t(one[k], two[k])
        return each * total

    def put_plain(slot, team, one):
        put_folded(slot, team, scale * nacc[team, slot] + own_part(team, one, one))

    def put_cross(slot, team, one, two):
        cross = scale * nacc[team, slot] + own_part(team, one, two)
        put_folded(slot, team, cross + cross.T)

    def norms(team):
        h_row = a_row = jnp.zeros((1, half), F32)
        for k in teams[team]:
            wide = vec[k].astype(F32)
            h_row = h_row + fold(wide * acc[k])
            a_row = a_row + fold(wide * wide)
        return h_row, a_row

    def level_of(rnd):
        total = column_of(scalar_wait(rnd, 0))
        h_here, a_here = total[0:1], total[1:2] * each
        some = a_here > 0.0
        return jnp.where(some, h_here / jnp.where(some, a_here, 1.0), 0.0)

    def correct(k, level, shard):
        held = vec[k, pl.ds(own_row, quarter), :].astype(F32)
        inside_k = jnp.where(mask_of(k, own_row, quarter), shard[0], 0.0)
        cor[k, pl.ds(own_row, quarter), :] = (inside_k - level * held).astype(BF16)

    acc_of = [acc.at[pl.ds(k, 1)] for k in range(3)]
    core_of = [core_a.at[pl.ds(k, 1)] for k in range(3)]
    half_of = [half_a.at[pl.ds(k, 1)] for k in range(3)]
    part_of = [part_a.at[k] for k in range(3)]
    cor_of = [cor.at[pl.ds(k, 1)] for k in range(3)]

    def arrive(t):
        for copy in ops_copies(t):
            copy.wait_recv()
        restore(t, got_l, sl1)
        restore(t, got_r, sr1)

    acc[...] = jnp.zeros_like(acc)
    acc_b[...] = jnp.zeros_like(acc_b)
    nacc[...] = jnp.zeros_like(nacc)

    @pl.loop(0, terms, unroll=True)
    def _(t):
        part_own(t, vec, img_a, acc)

    scatter_start(acc_of[0], core_of[0], 0)
    h_zero, a_zero = norms(0)
    scalar_start(0, 0, row_of([h_zero, a_zero]))
    psi_copy.wait_recv()
    gather_start(got_psi, 8)
    scatter_pass(acc_of[0], core_of[0], half_of[0], part_of[0], 0)

    @pl.loop(0, terms, unroll=True)
    def _(t):
        grow(0, 0, img_a, img_a, t)

    early = terms // 4
    for t in range(early):
        arrive(t)
        part_one(t, vec, img_a, acc)
    gather_pass(got_psi, 8)
    level_zero = level_of(0)
    shard = scatter_end(half_of[0], part_of[0], 0)
    correct(0, level_zero, shard)
    gather_start(cor_of[0], 9)
    gather_end(got_psi, 8)
    vec[2] = jnp.where(mask_of(2, 0, width), got_psi[...].astype(F32), 0.0).astype(BF16)
    for t in range(early):
        part_two(t, vec, img_a, acc)
    middle = terms // 2
    for t in range(early, middle):
        arrive(t)
        part_one(t, vec, img_a, acc)
        part_two(t, vec, img_a, acc)
    gather_pass(cor_of[0], 9)
    for t in range(middle, middle + 1):
        arrive(t)
        part_one(t, vec, img_a, acc)
        part_two(t, vec, img_a, acc)
    gather_end(cor_of[0], 9)

    @pl.loop(0, terms, unroll=True)
    def _(t):
        part_own(t, cor, img_b, acc_b)

    for t in range(middle + 1, terms):
        arrive(t)
        part_one(t, vec, img_a, acc)
        part_two(t, vec, img_a, acc)
    scatter_start(acc_of[1], core_of[1], 1)
    scatter_start(acc_of[2], core_of[2], 6)
    h_near, a_near = norms(1)
    scalar_start(1, 0, row_of([h_near, a_near]))

    @pl.loop(0, terms, unroll=True)
    def _(t):
        grow(1, 0, img_b, img_b, t)

    scatter_pass(acc_of[1], core_of[1], half_of[1], part_of[1], 1)
    scatter_pass(acc_of[2], core_of[2], half_of[2], part_of[2], 6)

    @pl.loop(0, terms, unroll=True)
    def _(t):
        grow(2, 0, img_a, img_b, t)

    put_plain(0, 0, vec)
    put_plain(1, 0, cor)
    put_cross(2, 0, vec, cor)
    scatter_start(mats.at[0], core_m.at[0], 2)
    level_near = level_of(1)
    shard = scatter_end(half_of[1], part_of[1], 1)
    correct(1, level_near, shard)
    gather_start(cor_of[1], 10)
    shard = scatter_end(half_of[2], part_of[2], 6)
    correct(2, level_near, shard)
    gather_start(cor_of[2], 7)

    @pl.loop(0, terms, unroll=True)
    def _(t):
        grow(0, 1, img_a, img_a, t)

    put_plain(0, 1, vec)
    scatter_start(mats.at[1, 0], core_m.at[1, 0], 3)
    gather_pass(cor_of[1], 10)
    gather_end(cor_of[1], 10)

    @pl.loop(0, middle, unroll=True)
    def _(t):
        part_one(t, cor, img_b, acc_b)

    gather_pass(cor_of[2], 7)

    @pl.loop(middle, terms, unroll=True)
    def _(t):
        part_one(t, cor, img_b, acc_b)

    gather_end(cor_of[2], 7)
    tag_out[...] = jnp.broadcast_to(level_near, (8, half))
    scatter_pass(mats.at[0], core_m.at[0], half_m.at[0], part_m, 2)

    @pl.loop(0, terms, unroll=True)
    def _(t):
        part_two(t, cor, img_b, acc_b)

    levels = [level_zero, level_near]
    sides = [(h_zero, a_zero), (h_near, a_near)]
    gathered = [jnp.zeros((1, half), F32)] * 6
    for team in range(2):
        level, (h_row, a_row) = levels[team], sides[team]
        vc = cc = vhc = chc = jnp.zeros((1, half), F32)
        for k in teams[team]:
            wide, corr = vec[k].astype(F32), cor[k].astype(F32)
            summed = acc_b[k]
            vc = vc + fold(wide * corr)
            cc = cc + fold(corr * corr)
            vhc = vhc + fold(wide * summed)
            chc = chc + fold(corr * summed)
        here = [
            a_row * each,
            h_row,
            (vc + level * a_row) * each,
            (cc + level * (2.0 * vc + level * a_row)) * each,
            vhc + level * h_row,
            chc + level * (2.0 * vhc + level * h_row),
        ]
        gathered = [one + two for one, two in zip(gathered, here)]
    scalar_start(2, 1, row_of(gathered))
    scatter_pass(mats.at[1, 0], core_m.at[1, 0], half_m.at[1, 0], part_n.at[0], 3)

    @pl.loop(0, terms, unroll=True)
    def _(t):
        grow(1, 1, img_b, img_b, t)

    put_plain(1, 1, cor)
    scatter_start(mats.at[1, 1], core_m.at[1, 1], 4)

    @pl.loop(0, terms, unroll=True)
    def _(t):
        grow(2, 1, img_a, img_b, t)

    put_cross(2, 1, vec, cor)
    scatter_start(mats.at[1, 2], core_m.at[1, 2], 5)
    scatter_pass(mats.at[1, 1], core_m.at[1, 1], half_m.at[1, 1], part_n.at[1], 4)
    scalar_start(2, 2, scalar_wait(2, 1))
    to_owner = [
        send(cor.at[2], cor_got, one_send.at[2], one_recv.at[2], down, lane),
        send(tag_out, tag_in, one_send.at[3], one_recv.at[3], down, lane),
    ]
    start(*to_owner)
    scatter_pass(mats.at[1, 2], core_m.at[1, 2], half_m.at[1, 2], part_n.at[2], 5)
    stay = scatter_end(half_m.at[0], part_m, 2)
    count = stay.shape[1]
    for q in range(3):
        hop_out[q * count:(q + 1) * count] = scatter_end(half_m.at[1, q], part_n.at[q], 3 + q)
    hop_out[3 * count:] = jnp.broadcast_to(level_near, (8, half))
    hop = send(hop_out, hop_in, one_send.at[1], one_recv.at[1], up, lane)
    start(hop)
    scalar_start(2, 0, scalar_wait(2, 2))
    whole = column_of(scalar_wait(2, 0))
    a11, h11, v_u, u_u, v_hu, u_hu = [whole[q:q + 1] for q in range(6)]
    mean = h11 / a11
    a12 = v_u - mean * a11
    a22 = u_u - mean * (2.0 * v_u - mean * a11)
    h12 = v_hu - mean * h11
    h22 = u_hu - mean * (2.0 * v_hu - mean * h11)
    quad_a = a11 * a22 - a12 * a12
    quad_b = h11 * a22 + h22 * a11 - 2.0 * h12 * a12
    quad_c = h11 * h22 - h12 * h12
    lowest = (quad_b - jnp.sqrt(jnp.maximum(quad_b * quad_b - 4.0 * quad_a * quad_c, 0.0))) / (
        2.0 * quad_a
    )
    ratio = (lowest * a11 - h11) / (h12 - lowest * a12)
    first_coef = lax.rsqrt(a11 + 2.0 * ratio * a12 + ratio * ratio * a22)
    second_coef = ratio * first_coef

    def weigh(coef, parts):
        return coef * coef * parts[0] + coef * second_coef * parts[2] + second_coef * second_coef * parts[1]

    coefs = [first_coef + second_coef * (level - mean) for level in levels]
    stay = weigh(coefs[0], [stay[q] for q in range(3)])
    hop.wait_recv()
    coef_last = first_coef + second_coef * (hop_in[3 * count:3 * count + 1, 0:1] - mean)
    come = weigh(coef_last, [hop_in[q * count:(q + 1) * count] for q in range(3)])
    piled = folded.at[pl.ds(0, 3 * half)]
    rows(piled, (c * xs + x) * count, count)[...] = stay + come
    gather_start(piled, 11)
    for copy in to_owner:
        copy.wait_recv()
    coefs.append(first_coef + second_coef * (tag_in[0:1, 0:1] - mean))
    rows_last = jnp.where(me + 2 < ns, left_dims[lax.rem(me + 2, ns)], 0)
    row = lax.broadcasted_iota(jnp.int32, (width, width), 0)
    col = lax.broadcasted_iota(jnp.int32, (width, width), 1)
    last = jnp.where((row < rows_last) & (col < cols_own), psi[2].astype(F32), 0.0)
    pairs = [(vec[k].astype(F32), cor[k].astype(F32)) for k in range(2)] + [(last, cor_got[...].astype(F32))]
    for k, (wide, corr) in enumerate(pairs):
        ns_mine[k] = (coefs[k] * wide + second_coef * corr).astype(BF16)
    tail = lax.broadcasted_iota(jnp.int32, (8, half), 0)
    live = jnp.broadcast_to(rows_own, (8, half)).astype(F32)
    folded[3 * half:] = jnp.where(tail == 0, live, lowest)
    state_copy = load(ns_mine, state_hbm, 7)
    state_copy.start()
    gather_pass(piled, 11)
    gather_end(piled, 11)
    folded_copy = load(folded, folded_hbm, 8)
    folded_copy.start()
    @pl.loop(0, terms)
    def _(t):
        for copy in ops_copies(t):
            copy.wait_send()

    for copy in waits:
        copy.wait_send()
    state_copy.wait()
    folded_copy.wait()


def sign_kernel(half, folded, state_hbm, new_state_hbm, kept, energy, state, sem):
    width = 2 * half
    into = pltpu.make_async_copy(state_hbm, state, sem.at[0])
    into.start()
    row = lax.broadcasted_iota(jnp.int32, (width, width), 0)
    col = lax.broadcasted_iota(jnp.int32, (width, width), 1)
    identity = jnp.where(row == col, 1.0, 0.0).astype(F32)
    live = folded[3 * half:3 * half + 1, 0:1]
    energy[...] = folded[3 * half + 1:3 * half + 2, 0:1]
    corner = folded[half:width]
    density = jnp.concatenate([
        jnp.concatenate([folded[:half], corner], axis=1),
        jnp.concatenate([corner.T, folded[width:3 * half]], axis=1),
    ], axis=0)
    inside = (row.astype(F32) < live) & (col.astype(F32) < live)
    density = jnp.where(inside, density, 0.0)
    trace = jnp.sum(jnp.sum(density * identity, axis=0, keepdims=True), axis=1, keepdims=True)
    shifted = density - (trace / live) * identity
    square = jnp.sum(jnp.sum(shifted * shifted, axis=0, keepdims=True), axis=1, keepdims=True)
    kept[...] = shifted / jnp.sqrt(square)
    out = pltpu.make_async_copy(state, new_state_hbm, sem.at[1])

    def step():
        current = kept[...]
        parts = halves(current)
        squared = dot_wide(parts, parts)
        cubed = dot_wide(halves(squared), parts)
        kept[...] = 1.5 * current - 0.5 * cubed

    pl.loop(0, SIGN_STEPS // 2)(lambda _: step())
    into.wait()
    out.start()
    pl.loop(SIGN_STEPS // 2, SIGN_STEPS)(lambda _: step())
    kept[...] = 0.5 * (identity + kept[...])
    out.wait()


def per_device(zs, ns, tg, psi, left_ops, right_ops, left_dims, right_dims):
    terms, width = left_ops.shape[0], left_ops.shape[-1]
    half, xs = width // 2, tg // CORES
    quarter, ys = half // xs, ns // zs
    tall = 3 * half
    share = tall // 2 // xs
    most = max(tg, zs, ys)
    vmem, hbm = pl.BlockSpec(memory_space=pltpu.VMEM), pl.BlockSpec(memory_space=pltpu.HBM)
    dma = pltpu.SemaphoreType.DMA
    state, folded = pl.pallas_call(
        functools.partial(kernel, (ns, zs, tg, terms, width)),
        out_shape=(
            jax.ShapeDtypeStruct((3, width, width), BF16),
            jax.ShapeDtypeStruct((tall + 8, half), F32),
        ),
        in_specs=[hbm] * 5,
        out_specs=(hbm, hbm),
        scratch_shapes=[pltpu.SMEM((ns,), jnp.int32)] * 2
        + [pltpu.VMEM((3, width, width), BF16)]
        + [pltpu.VMEM((terms, width, width), BF16)] * 6
        + [pltpu.VMEM((terms, width + 8, half), BF16)] * 4
        + [pltpu.VMEM((width, width), BF16)]
        + [pltpu.VMEM((3, width, width), BF16)] * 2
        + [pltpu.VMEM((terms, 3, width, width), BF16)] * 2
        + [pltpu.VMEM((3, width, width), F32)] * 2
        + [pltpu.VMEM((3, half, width), F32)] * 2
        + [pltpu.VMEM((3, xs, 1, quarter, width), F32)]
        + [pltpu.VMEM((2, 3, width, width), F32)]
        + [pltpu.VMEM((2, 3, tall, half), F32)]
        + [pltpu.VMEM((2, 3, tall // 2, half), F32)] * 2
        + [pltpu.VMEM((xs, 3, share, half), F32)]
        + [pltpu.VMEM((3, xs, share, half), F32)]
        + [pltpu.VMEM((3 * share + 8, half), F32)] * 2
        + [pltpu.VMEM((tall + 8, half), F32)]
        + [pltpu.VMEM((3, 3, most, 1, half), F32)]
        + [pltpu.VMEM((3, width, width), BF16), pltpu.VMEM((width, width), BF16)]
        + [pltpu.VMEM((8, half), F32)] * 2
        + [dma((9,)), dma((2, terms)), dma((2, terms)), dma((4,)), dma((4,))]
        + [dma((12, xs))] * 4
        + [dma((3, 3, most))] * 2,
        compiler_params=pltpu.CompilerParams(
            collective_id=0, has_side_effects=True, vmem_limit_bytes=67043328
        ),
    )(left_dims, right_dims, psi[0], left_ops[:, 0], right_ops[:, 0])
    new_state, kept, energy = pl.pallas_call(
        functools.partial(sign_kernel, half),
        out_shape=(
            jax.ShapeDtypeStruct((3, width, width), BF16),
            jax.ShapeDtypeStruct((width, width), F32),
            jax.ShapeDtypeStruct((1, 1), F32),
        ),
        in_specs=[vmem, hbm],
        out_specs=(hbm, vmem, vmem),
        scratch_shapes=[pltpu.VMEM((3, width, width), BF16), dma((2,))],
    )(folded, state)
    return new_state[None], kept[None], energy[0, 0]


def solution(mesh):
    ns, tg = mesh.shape["sec"], mesh.shape["term"]
    zs = ZSIZE if ns % ZSIZE == 0 and ns > ZSIZE else 2
    in_specs = (
        P("sec", None, None, None),
        P("term", "sec", None, None),
        P("term", "sec", None, None),
        P(),
        P(),
    )
    out_specs = (P("sec", None, None, None), P("sec", None, None), P())
    return jax.shard_map(
        functools.partial(per_device, zs, ns, tg),
        mesh=mesh, in_specs=in_specs, out_specs=out_specs, check_vma=False,
    )
```

```python
import functools

import jax
import jax.numpy as jnp
from jax import lax
from jax.experimental import pallas as pl
from jax.experimental.pallas import tpu as pltpu
from jax.sharding import PartitionSpec as P

SIGN_STEPS = 6
ZSIZE = 8
CORES = 2
NOISE_WEIGHT = 0.5
MESH = pl.DeviceIdType.MESH
F32 = jnp.float32
BF16 = jnp.bfloat16


def dot(a, b):
    return jnp.dot(a, b, preferred_element_type=F32)


def dot_t(a, b):
    return lax.dot_general(a, b, (((1,), (1,)), ((), ())), preferred_element_type=F32)


def halves(value):
    high = value.astype(BF16)
    return high, (value - high.astype(F32)).astype(BF16)


def dot_wide(a, b):
    (ah, al), (bh, bl) = a, b
    return dot(jnp.concatenate([ah, ah, al], axis=1), jnp.concatenate([bh, bl, bh], axis=0))


def fold(value):
    half = value.shape[1] // 2
    row = jnp.sum(value, axis=0, keepdims=True)
    return row[:, :half] + row[:, half:]


def kernel(
    sizes,
    left_dims_hbm, right_dims_hbm, psi_hbm, left_hbm, right_hbm,
    state_hbm, folded_hbm,
    left_dims, right_dims, psi, left, right,
    sl0, sr0, sl1, sr1, pack_l, pack_r, got_l, got_r, got_psi,
    vec, cor, img_a, img_b, acc, acc_b, core_a, half_a, part_a,
    nacc, mats, core_m, half_m, part_m, part_n, hop_out, hop_in, folded,
    sums, ns_mine, cor_got, tag_out, tag_in,
    in_sem, pack_send, pack_recv, one_send, one_recv, c_send, c_recv, x_send, x_recv, s_send, s_recv, chain,
):
    ns, zs, tg, terms, width = sizes
    ys, xs = ns // zs, tg // CORES
    half = width // 2
    me, lane = lax.axis_index("sec"), lax.axis_index("term")
    x, c = lax.div(lane, CORES), lax.rem(lane, CORES)
    y, z = lax.div(me, zs), lax.rem(me, zs)
    up, down = lax.rem(me + 1, ns), lax.rem(me + ns - 1, ns)
    partner = lane + 1 - 2 * c
    far_first = sorted(range(1, xs), key=lambda d: -min(d, xs - d))
    order = [lax.rem(x + d, xs) for d in far_first] + [x]

    def send(src, dst, ssem, rsem, sec, term):
        return pltpu.make_async_remote_copy(
            src_ref=src, dst_ref=dst, send_sem=ssem, recv_sem=rsem,
            device_id=(sec, term), device_id_type=MESH,
        )

    barrier = pltpu.get_barrier_semaphore()
    groups = [
        [((me, lax.rem(lane + d, tg)), lax.rem(lane + d, tg)) for d in range(1, tg)],
        [((y * zs + lax.rem(z + d, zs), lane), lax.rem(z + d, zs)) for d in range(1, zs)],
        [((lax.rem(y + d, ys) * zs + z, lane), lax.rem(y + d, ys)) for d in range(1, ys)],
    ]
    places = [lane, z, y]
    rings = [
        [(y * zs + lax.rem(z + 1, zs), lane), (y * zs + lax.rem(z + zs - 1, zs), lane)],
        [(lax.rem(y + 1, ys) * zs + z, lane), (lax.rem(y + ys - 1, ys) * zs + z, lane)],
    ]
    reach = [zs // 2 - 1, ys // 2 - 1]
    greeted = [peer for peer, _ in groups[0]] + rings[0] + rings[1] + [(up, lane), (down, lane)]
    for peer in greeted:
        pl.semaphore_signal(barrier, inc=1, device_id=peer, device_id_type=MESH)

    def vouch(turn):
        for axis in range(2):
            if turn < reach[axis]:
                for side, peer in enumerate(rings[axis]):
                    pl.semaphore_signal(
                        chain.at[axis, turn, side], inc=1, device_id=peer, device_id_type=MESH
                    )

    def vouched(turn):
        for axis in range(2):
            if turn < reach[axis]:
                for side in range(2):
                    pl.semaphore_wait(chain.at[axis, turn, side], 1)

    def load(src, dst, slot):
        return pltpu.make_async_copy(src, dst, in_sem.at[slot])

    rest = pl.ds(1, terms - 1)
    loads = [
        load(left_hbm.at[0], left.at[0], 0),
        load(right_hbm.at[0], right.at[0], 1),
        load(psi_hbm, psi, 2),
        load(left_hbm.at[rest], left.at[rest], 3),
        load(right_hbm.at[rest], right.at[rest], 4),
        load(left_dims_hbm, left_dims, 5),
        load(right_dims_hbm, right_dims, 6),
    ]
    for copy in loads:
        copy.start()

    row_h = lax.broadcasted_iota(jnp.int32, (half, half), 0)
    col_h = lax.broadcasted_iota(jnp.int32, (half, half), 1)

    def prepare(t, raw, sym, pack):
        wide = raw[t].astype(F32)
        whole = (wide + wide.T).astype(BF16)
        sym[t] = whole
        again = whole.astype(F32)
        low, high = again[:half, :half], again[half:, half:]
        pack[t, :half] = whole[:half, half:]
        pack[t, half:width] = jnp.where(row_h <= col_h, low, high).astype(BF16)
        diag = jnp.sum(jnp.where(row_h == col_h, high, 0.0), axis=0, keepdims=True)
        pack[t, width:] = jnp.broadcast_to(diag, (8, half)).astype(BF16)

    def restore(t, pack, sym):
        corner = pack[t, :half].astype(F32)
        mixed = pack[t, half:width].astype(F32)
        diag = pack[t, width:].astype(F32)[0:1]
        turned = mixed.T
        sym[t, :half, :half] = jnp.where(row_h <= col_h, mixed, turned).astype(BF16)
        sym[t, :half, half:] = pack[t, :half]
        sym[t, half:, :half] = corner.T.astype(BF16)
        lower = jnp.where(row_h == col_h, jnp.broadcast_to(diag, (half, half)), turned)
        sym[t, half:, half:] = jnp.where(row_h > col_h, mixed, lower).astype(BF16)

    def ops_copies(t):
        return (
            send(pack_l.at[t], got_l.at[t], pack_send.at[0, t], pack_recv.at[0, t], down, lane),
            send(pack_r.at[t], got_r.at[t], pack_send.at[1, t], pack_recv.at[1, t], up, lane),
        )

    def prepare_both(t):
        prepare(t, left, sl0, pack_l)
        prepare(t, right, sr0, pack_r)

    waits = []

    def start(*copies):
        for copy in copies:
            copy.start()
        waits.extend(copies)

    def rows(ref, first, count):
        return ref.at[..., pl.ds(pl.multiple_of(first, count), count), :]

    def gather_start(ref, slot):
        hr, qr = ref.shape[-2] // 2, ref.shape[-2] // 2 // xs
        own = rows(ref, c * hr + x * qr, qr)
        for i, d in enumerate(far_first):
            start(send(own, own, x_send.at[slot, i], x_recv.at[slot, x], me, order[i] * CORES + c))
        start(send(own, own, c_send.at[slot, x], c_recv.at[slot, x], me, partner))

    def gather_pass(ref, slot):
        hr, qr = ref.shape[-2] // 2, ref.shape[-2] // 2 // xs
        for i in reversed(range(len(far_first))):
            piece = rows(ref, c * hr + order[i] * qr, qr)
            send(
                piece, piece, x_send.at[slot, i], x_recv.at[slot, order[i]], me, order[i] * CORES + c
            ).wait_recv()
            start(send(piece, piece, c_send.at[slot, order[i]], c_recv.at[slot, order[i]], me, partner))

    def gather_end(ref, slot):
        hr, qr = ref.shape[-2] // 2, ref.shape[-2] // 2 // xs
        for i in range(xs):
            piece = rows(ref, (1 - c) * hr + i * qr, qr)
            send(piece, piece, c_send.at[slot, i], c_recv.at[slot, i], me, partner).wait_recv()

    def core_copies(buf, core, slot):
        hr, qr = core.shape[-2], core.shape[-2] // xs
        return [
            send(
                rows(buf, (1 - c) * hr + xi * qr, qr), rows(core, xi * qr, qr),
                c_send.at[slot, i], c_recv.at[slot, i], me, partner,
            )
            for i, xi in enumerate(order)
        ]

    def scatter_start(buf, core, slot):
        start(*core_copies(buf, core, slot))

    def scatter_pass(buf, core, halved, part, slot):
        hr, qr = core.shape[-2], core.shape[-2] // xs
        copies = core_copies(buf, core, slot)
        late = None
        for i, xi in enumerate(order):
            copies[i].wait_recv()
            mine = rows(buf, c * hr + xi * qr, qr)[...] + rows(core, xi * qr, qr)[...]
            if i < xs - 1:
                piece = rows(halved, xi * qr, qr)
                piece[...] = mine
                now = send(
                    piece, part.at[x], x_send.at[slot, i], x_recv.at[slot, x], me, xi * CORES + c
                )
            else:
                part[x] = mine
                now = None
            if late is not None:
                start(late)
            late = now

    def scatter_end(halved, part, slot):
        qr = halved.shape[-2] // xs
        for i in range(xs - 1):
            send(
                rows(halved, order[i] * qr, qr), part.at[order[i]],
                x_send.at[slot, i], x_recv.at[slot, order[i]], me, order[i] * CORES + c,
            ).wait_recv()
        total = part[0]
        for i in range(1, xs):
            total = total + part[i]
        return total

    def scalar_start(rnd, stage, value):
        sums[rnd, stage, places[stage]] = value
        own = sums.at[rnd, stage, places[stage]]
        for d, (peer, _) in enumerate(groups[stage]):
            start(send(own, own, s_send.at[rnd, stage, d], s_recv.at[rnd, stage, places[stage]], *peer))

    def scalar_wait(rnd, stage):
        for d, (peer, place) in enumerate(groups[stage]):
            slot = sums.at[rnd, stage, place]
            send(slot, slot, s_send.at[rnd, stage, d], s_recv.at[rnd, stage, place], *peer).wait_recv()
        total = sums[rnd, stage, 0]
        for i in range(1, len(groups[stage]) + 1):
            total = total + sums[rnd, stage, i]
        return total

    one_hot = lax.broadcasted_iota(jnp.int32, (8, half), 0) == lax.broadcasted_iota(jnp.int32, (8, half), 1)

    def row_of(values):
        values = jnp.concatenate(values + [jnp.zeros((8 - len(values), half), F32)], axis=0)
        full = jnp.broadcast_to(jnp.sum(values, axis=1, keepdims=True), (8, half))
        return jnp.sum(jnp.where(one_hot, full, 0.0), axis=0, keepdims=True)

    def column_of(row):
        return jnp.sum(jnp.where(one_hot, jnp.broadcast_to(row, (8, half)), 0.0), axis=1, keepdims=True)

    loads[0].wait()
    loads[1].wait()
    prepare_both(0)
    loads[2].wait()
    pl.semaphore_wait(barrier, len(greeted))
    vouch(0)
    psi_rows = width // tg
    psi_piece = rows(got_psi, c * half + x * psi_rows, psi_rows)
    psi_copy = send(
        rows(psi.at[2], c * half + x * psi_rows, psi_rows), psi_piece,
        one_send.at[0], one_recv.at[0], up, lane,
    )
    start(psi_copy)
    for copy in loads[3:]:
        copy.wait()

    @pl.loop(1, terms)
    def _(t):
        prepare_both(t)
        for copy in ops_copies(t - 1):
            copy.start()

    rows_own = left_dims[me]
    rows_next = jnp.where(me + 1 < ns, left_dims[up], 0)
    cols_own = right_dims[me]
    cols_last = jnp.where(me >= 1, right_dims[down], 0)
    live_rows = [rows_own, rows_next, rows_next]
    live_cols = [cols_own, cols_own, cols_last]

    def mask_of(k, first_row, count):
        row = lax.broadcasted_iota(jnp.int32, (count, width), 0) + first_row
        col = lax.broadcasted_iota(jnp.int32, (count, width), 1)
        return (row < live_rows[k]) & (col < live_cols[k])

    for k in range(2):
        vec[k] = jnp.where(mask_of(k, 0, width), psi[k].astype(F32), 0.0).astype(BF16)
    for copy in ops_copies(terms - 1):
        copy.start()

    scale, each = NOISE_WEIGHT / (terms * tg), 1.0 / tg
    quarter = half // xs
    own_row = pl.multiple_of(c * half + x * quarter, quarter)
    teams = [(0,), (1, 2)]

    def part_own(t, blocks, images, total):
        image = dot(sl0[t], blocks[0]).astype(BF16)
        images[t, 0] = image
        total[0] += dot(image, sr0[t])

    def part_one(t, blocks, images, total):
        image = dot(sl1[t], blocks[1]).astype(BF16)
        images[t, 1] = image
        total[1] += dot(image, sr0[t])

    def part_two(t, blocks, images, total):
        image = dot(sl1[t], blocks[2]).astype(BF16)
        images[t, 2] = image
        total[2] += dot(image, sr1[t])

    def grow(slot, team, one, two, t):
        for k in teams[team]:
            nacc[team, slot] += dot_t(one[t, k], two[t, k])

    def put_folded(slot, team, full):
        mats[team, slot, :half] = full[:half, :half]
        mats[team, slot, half:width] = full[:half, half:]
        mats[team, slot, width:] = full[half:, half:]

    def own_part(team, one, two):
        total = dot_t(one[teams[team][0]], two[teams[team][0]])
        for k in teams[team][1:]:
            total = total + dot_t(one[k], two[k])
        return each * total

    def put_plain(slot, team, one):
        put_folded(slot, team, scale * nacc[team, slot] + own_part(team, one, one))

    def put_cross(slot, team, one, two):
        cross = scale * nacc[team, slot] + own_part(team, one, two)
        put_folded(slot, team, cross + cross.T)

    def norms(team):
        h_row = a_row = jnp.zeros((1, half), F32)
        for k in teams[team]:
            wide = vec[k].astype(F32)
            h_row = h_row + fold(wide * acc[k])
            a_row = a_row + fold(wide * wide)
        return h_row, a_row

    def level_of(rnd):
        total = column_of(scalar_wait(rnd, 0))
        h_here, a_here = total[0:1], total[1:2] * each
        some = a_here > 0.0
        return jnp.where(some, h_here / jnp.where(some, a_here, 1.0), 0.0)

    def correct(k, level, shard):
        held = vec[k, pl.ds(own_row, quarter), :].astype(F32)
        inside_k = jnp.where(mask_of(k, own_row, quarter), shard[0], 0.0)
        cor[k, pl.ds(own_row, quarter), :] = (inside_k - level * held).astype(BF16)

    acc_of = [acc.at[pl.ds(k, 1)] for k in range(3)]
    core_of = [core_a.at[pl.ds(k, 1)] for k in range(3)]
    half_of = [half_a.at[pl.ds(k, 1)] for k in range(3)]
    part_of = [part_a.at[k] for k in range(3)]
    cor_of = [cor.at[pl.ds(k, 1)] for k in range(3)]

    def arrive(t):
        for copy in ops_copies(t):
            copy.wait_recv()
        restore(t, got_l, sl1)
        restore(t, got_r, sr1)

    acc[...] = jnp.zeros_like(acc)
    acc_b[...] = jnp.zeros_like(acc_b)
    nacc[...] = jnp.zeros_like(nacc)

    @pl.loop(0, terms, unroll=True)
    def _(t):
        part_own(t, vec, img_a, acc)

    scatter_start(acc_of[0], core_of[0], 0)
    h_zero, a_zero = norms(0)
    scalar_start(0, 0, row_of([h_zero, a_zero]))
    psi_copy.wait_recv()
    gather_start(got_psi, 8)
    scatter_pass(acc_of[0], core_of[0], half_of[0], part_of[0], 0)

    @pl.loop(0, terms, unroll=True)
    def _(t):
        grow(0, 0, img_a, img_a, t)

    early = terms // 4
    for t in range(early):
        arrive(t)
        part_one(t, vec, img_a, acc)
    vouched(0)
    vouch(1)
    gather_pass(got_psi, 8)
    level_zero = level_of(0)
    shard = scatter_end(half_of[0], part_of[0], 0)
    correct(0, level_zero, shard)
    gather_start(cor_of[0], 9)
    gather_end(got_psi, 8)
    vec[2] = jnp.where(mask_of(2, 0, width), got_psi[...].astype(F32), 0.0).astype(BF16)
    for t in range(early):
        part_two(t, vec, img_a, acc)
    middle = terms // 2
    for t in range(early, middle):
        arrive(t)
        part_one(t, vec, img_a, acc)
        part_two(t, vec, img_a, acc)
    vouched(1)
    vouch(2)
    gather_pass(cor_of[0], 9)
    for t in range(middle, middle + 1):
        arrive(t)
        part_one(t, vec, img_a, acc)
        part_two(t, vec, img_a, acc)
    gather_end(cor_of[0], 9)

    @pl.loop(0, terms, unroll=True)
    def _(t):
        part_own(t, cor, img_b, acc_b)

    for turn in range(2, max(reach)):
        vouched(turn)
        vouch(turn + 1)
    for t in range(middle + 1, terms):
        arrive(t)
        part_one(t, vec, img_a, acc)
        part_two(t, vec, img_a, acc)
    scatter_start(acc_of[1], core_of[1], 1)
    scatter_start(acc_of[2], core_of[2], 6)
    h_near, a_near = norms(1)
    scalar_start(1, 0, row_of([h_near, a_near]))

    @pl.loop(0, terms, unroll=True)
    def _(t):
        grow(1, 0, img_b, img_b, t)

    scatter_pass(acc_of[1], core_of[1], half_of[1], part_of[1], 1)
    scatter_pass(acc_of[2], core_of[2], half_of[2], part_of[2], 6)

    @pl.loop(0, terms, unroll=True)
    def _(t):
        grow(2, 0, img_a, img_b, t)

    put_plain(0, 0, vec)
    put_plain(1, 0, cor)
    put_cross(2, 0, vec, cor)
    scatter_start(mats.at[0], core_m.at[0], 2)
    level_near = level_of(1)
    shard = scatter_end(half_of[1], part_of[1], 1)
    correct(1, level_near, shard)
    gather_start(cor_of[1], 10)
    shard = scatter_end(half_of[2], part_of[2], 6)
    correct(2, level_near, shard)
    gather_start(cor_of[2], 7)

    @pl.loop(0, terms, unroll=True)
    def _(t):
        grow(0, 1, img_a, img_a, t)

    put_plain(0, 1, vec)
    scatter_start(mats.at[1, 0], core_m.at[1, 0], 3)
    gather_pass(cor_of[1], 10)
    gather_end(cor_of[1], 10)

    @pl.loop(0, terms, unroll=True)
    def _(t):
        part_one(t, cor, img_b, acc_b)

    gather_pass(cor_of[2], 7)

    @pl.loop(0, terms, unroll=True)
    def _(t):
        nacc[1, 1] += dot_t(img_b[t, 1], img_b[t, 1])

    gather_end(cor_of[2], 7)
    tag_out[...] = jnp.broadcast_to(level_near, (8, half))
    scatter_pass(mats.at[0], core_m.at[0], half_m.at[0], part_m, 2)

    @pl.loop(0, terms, unroll=True)
    def _(t):
        part_two(t, cor, img_b, acc_b)

    levels = [level_zero, level_near]
    sides = [(h_zero, a_zero), (h_near, a_near)]
    gathered = [jnp.zeros((1, half), F32)] * 6
    for team in range(2):
        level, (h_row, a_row) = levels[team], sides[team]
        vc = cc = vhc = chc = jnp.zeros((1, half), F32)
        for k in teams[team]:
            wide, corr = vec[k].astype(F32), cor[k].astype(F32)
            summed = acc_b[k]
            vc = vc + fold(wide * corr)
            cc = cc + fold(corr * corr)
            vhc = vhc + fold(wide * summed)
            chc = chc + fold(corr * summed)
        here = [
            a_row * each,
            h_row,
            (vc + level * a_row) * each,
            (cc + level * (2.0 * vc + level * a_row)) * each,
            vhc + level * h_row,
            chc + level * (2.0 * vhc + level * h_row),
        ]
        gathered = [one + two for one, two in zip(gathered, here)]
    scalar_start(2, 1, row_of(gathered))
    scatter_pass(mats.at[1, 0], core_m.at[1, 0], half_m.at[1, 0], part_n.at[0], 3)

    @pl.loop(0, terms, unroll=True)
    def _(t):
        nacc[1, 1] += dot_t(img_b[t, 2], img_b[t, 2])

    put_plain(1, 1, cor)
    scatter_start(mats.at[1, 1], core_m.at[1, 1], 4)

    @pl.loop(0, terms, unroll=True)
    def _(t):
        grow(2, 1, img_a, img_b, t)

    put_cross(2, 1, vec, cor)
    scatter_start(mats.at[1, 2], core_m.at[1, 2], 5)
    scatter_pass(mats.at[1, 1], core_m.at[1, 1], half_m.at[1, 1], part_n.at[1], 4)
    scalar_start(2, 2, scalar_wait(2, 1))
    to_owner = [
        send(cor.at[2], cor_got, one_send.at[2], one_recv.at[2], down, lane),
        send(tag_out, tag_in, one_send.at[3], one_recv.at[3], down, lane),
    ]
    start(*to_owner)
    scatter_pass(mats.at[1, 2], core_m.at[1, 2], half_m.at[1, 2], part_n.at[2], 5)
    scalar_start(2, 0, scalar_wait(2, 2))
    stay = scatter_end(half_m.at[0], part_m, 2)
    count = stay.shape[1]
    for q in range(3):
        hop_out[q * count:(q + 1) * count] = scatter_end(half_m.at[1, q], part_n.at[q], 3 + q)
    hop_out[3 * count:] = jnp.broadcast_to(level_near, (8, half))
    hop = send(hop_out, hop_in, one_send.at[1], one_recv.at[1], up, lane)
    start(hop)
    whole = column_of(scalar_wait(2, 0))
    a11, h11, v_u, u_u, v_hu, u_hu = [whole[q:q + 1] for q in range(6)]
    mean = h11 / a11
    a12 = v_u - mean * a11
    a22 = u_u - mean * (2.0 * v_u - mean * a11)
    h12 = v_hu - mean * h11
    h22 = u_hu - mean * (2.0 * v_hu - mean * h11)
    quad_a = a11 * a22 - a12 * a12
    quad_b = h11 * a22 + h22 * a11 - 2.0 * h12 * a12
    quad_c = h11 * h22 - h12 * h12
    lowest = (quad_b - jnp.sqrt(jnp.maximum(quad_b * quad_b - 4.0 * quad_a * quad_c, 0.0))) / (
        2.0 * quad_a
    )
    ratio = (lowest * a11 - h11) / (h12 - lowest * a12)
    first_coef = lax.rsqrt(a11 + 2.0 * ratio * a12 + ratio * ratio * a22)
    second_coef = ratio * first_coef

    def weigh(coef, parts):
        return coef * coef * parts[0] + coef * second_coef * parts[2] + second_coef * second_coef * parts[1]

    coefs = [first_coef + second_coef * (level - mean) for level in levels]
    stay = weigh(coefs[0], [stay[q] for q in range(3)])
    hop.wait_recv()
    coef_last = first_coef + second_coef * (hop_in[3 * count:3 * count + 1, 0:1] - mean)
    come = weigh(coef_last, [hop_in[q * count:(q + 1) * count] for q in range(3)])
    piled = folded.at[pl.ds(0, 3 * half)]
    rows(piled, (c * xs + x) * count, count)[...] = stay + come
    gather_start(piled, 11)
    for copy in to_owner:
        copy.wait_recv()
    coefs.append(first_coef + second_coef * (tag_in[0:1, 0:1] - mean))
    rows_last = jnp.where(me + 2 < ns, left_dims[lax.rem(me + 2, ns)], 0)
    row = lax.broadcasted_iota(jnp.int32, (width, width), 0)
    col = lax.broadcasted_iota(jnp.int32, (width, width), 1)
    last = jnp.where((row < rows_last) & (col < cols_own), psi[2].astype(F32), 0.0)
    pairs = [(vec[k].astype(F32), cor[k].astype(F32)) for k in range(2)] + [(last, cor_got[...].astype(F32))]
    for k, (wide, corr) in enumerate(pairs):
        ns_mine[k] = (coefs[k] * wide + second_coef * corr).astype(BF16)
    tail = lax.broadcasted_iota(jnp.int32, (8, half), 0)
    live = jnp.broadcast_to(rows_own, (8, half)).astype(F32)
    folded[3 * half:] = jnp.where(tail == 0, live, lowest)
    state_copy = load(ns_mine, state_hbm, 7)
    state_copy.start()
    gather_pass(piled, 11)
    gather_end(piled, 11)
    folded_copy = load(folded, folded_hbm, 8)
    folded_copy.start()
    @pl.loop(0, terms)
    def _(t):
        for copy in ops_copies(t):
            copy.wait_send()

    for copy in waits:
        copy.wait_send()
    state_copy.wait()
    folded_copy.wait()


def sign_kernel(half, folded, state_hbm, new_state_hbm, kept, energy, state, sem):
    width = 2 * half
    into = pltpu.make_async_copy(state_hbm, state, sem.at[0])
    into.start()
    row = lax.broadcasted_iota(jnp.int32, (width, width), 0)
    col = lax.broadcasted_iota(jnp.int32, (width, width), 1)
    identity = jnp.where(row == col, 1.0, 0.0).astype(F32)
    live = folded[3 * half:3 * half + 1, 0:1]
    energy[...] = folded[3 * half + 1:3 * half + 2, 0:1]
    corner = folded[half:width]
    density = jnp.concatenate([
        jnp.concatenate([folded[:half], corner], axis=1),
        jnp.concatenate([corner.T, folded[width:3 * half]], axis=1),
    ], axis=0)
    inside = (row.astype(F32) < live) & (col.astype(F32) < live)
    density = jnp.where(inside, density, 0.0)
    trace = jnp.sum(jnp.sum(density * identity, axis=0, keepdims=True), axis=1, keepdims=True)
    shifted = density - (trace / live) * identity
    square = jnp.sum(jnp.sum(shifted * shifted, axis=0, keepdims=True), axis=1, keepdims=True)
    kept[...] = shifted / jnp.sqrt(square)
    out = pltpu.make_async_copy(state, new_state_hbm, sem.at[1])

    def step():
        current = kept[...]
        parts = halves(current)
        squared = dot_wide(parts, parts)
        cubed = dot_wide(halves(squared), parts)
        kept[...] = 1.5 * current - 0.5 * cubed

    pl.loop(0, SIGN_STEPS // 2)(lambda _: step())
    into.wait()
    out.start()
    pl.loop(SIGN_STEPS // 2, SIGN_STEPS)(lambda _: step())
    kept[...] = 0.5 * (identity + kept[...])
    out.wait()


def per_device(zs, ns, tg, psi, left_ops, right_ops, left_dims, right_dims):
    terms, width = left_ops.shape[0], left_ops.shape[-1]
    half, xs = width // 2, tg // CORES
    quarter, ys = half // xs, ns // zs
    tall = 3 * half
    share = tall // 2 // xs
    most = max(tg, zs, ys)
    vmem, hbm = pl.BlockSpec(memory_space=pltpu.VMEM), pl.BlockSpec(memory_space=pltpu.HBM)
    dma = pltpu.SemaphoreType.DMA
    state, folded = pl.pallas_call(
        functools.partial(kernel, (ns, zs, tg, terms, width)),
        out_shape=(
            jax.ShapeDtypeStruct((3, width, width), BF16),
            jax.ShapeDtypeStruct((tall + 8, half), F32),
        ),
        in_specs=[hbm] * 5,
        out_specs=(hbm, hbm),
        scratch_shapes=[pltpu.SMEM((ns,), jnp.int32)] * 2
        + [pltpu.VMEM((3, width, width), BF16)]
        + [pltpu.VMEM((terms, width, width), BF16)] * 6
        + [pltpu.VMEM((terms, width + 8, half), BF16)] * 4
        + [pltpu.VMEM((width, width), BF16)]
        + [pltpu.VMEM((3, width, width), BF16)] * 2
        + [pltpu.VMEM((terms, 3, width, width), BF16)] * 2
        + [pltpu.VMEM((3, width, width), F32)] * 2
        + [pltpu.VMEM((3, half, width), F32)] * 2
        + [pltpu.VMEM((3, xs, 1, quarter, width), F32)]
        + [pltpu.VMEM((2, 3, width, width), F32)]
        + [pltpu.VMEM((2, 3, tall, half), F32)]
        + [pltpu.VMEM((2, 3, tall // 2, half), F32)] * 2
        + [pltpu.VMEM((xs, 3, share, half), F32)]
        + [pltpu.VMEM((3, xs, share, half), F32)]
        + [pltpu.VMEM((3 * share + 8, half), F32)] * 2
        + [pltpu.VMEM((tall + 8, half), F32)]
        + [pltpu.VMEM((3, 3, most, 1, half), F32)]
        + [pltpu.VMEM((3, width, width), BF16), pltpu.VMEM((width, width), BF16)]
        + [pltpu.VMEM((8, half), F32)] * 2
        + [dma((9,)), dma((2, terms)), dma((2, terms)), dma((4,)), dma((4,))]
        + [dma((12, xs))] * 4
        + [dma((3, 3, most))] * 2
        + [pltpu.SemaphoreType.REGULAR((2, max(zs // 2, ys // 2), 2))],
        compiler_params=pltpu.CompilerParams(
            collective_id=0, has_side_effects=True, vmem_limit_bytes=67043328
        ),
    )(left_dims, right_dims, psi[0], left_ops[:, 0], right_ops[:, 0])
    new_state, kept, energy = pl.pallas_call(
        functools.partial(sign_kernel, half),
        out_shape=(
            jax.ShapeDtypeStruct((3, width, width), BF16),
            jax.ShapeDtypeStruct((width, width), F32),
            jax.ShapeDtypeStruct((1, 1), F32),
        ),
        in_specs=[vmem, hbm],
        out_specs=(hbm, vmem, vmem),
        scratch_shapes=[pltpu.VMEM((3, width, width), BF16), dma((2,))],
    )(folded, state)
    return new_state[None], kept[None], energy[0, 0]


def solution(mesh):
    ns, tg = mesh.shape["sec"], mesh.shape["term"]
    zs = ZSIZE if ns % ZSIZE == 0 and ns > ZSIZE else 2
    in_specs = (
        P("sec", None, None, None),
        P("term", "sec", None, None),
        P("term", "sec", None, None),
        P(),
        P(),
    )
    out_specs = (P("sec", None, None, None), P("sec", None, None), P())
    return jax.shard_map(
        functools.partial(per_device, zs, ns, tg),
        mesh=mesh, in_specs=in_specs, out_specs=out_specs, check_vma=False,
    )
```

```python
import functools

import jax
import jax.numpy as jnp
from jax import lax
from jax.experimental import pallas as pl
from jax.experimental.pallas import tpu as pltpu
from jax.sharding import PartitionSpec as P

SIGN_STEPS = 6
ZSIZE = 8
CORES = 2
NOISE_WEIGHT = 0.5
MESH = pl.DeviceIdType.MESH
F32 = jnp.float32
BF16 = jnp.bfloat16


def dot(a, b):
    return jnp.dot(a, b, preferred_element_type=F32)


def dot_t(a, b):
    return lax.dot_general(a, b, (((1,), (1,)), ((), ())), preferred_element_type=F32)


def halves(value):
    high = value.astype(BF16)
    return high, (value - high.astype(F32)).astype(BF16)


def beside(high, low):
    return jnp.concatenate([high, high, low], axis=1)


def fold(value):
    half = value.shape[1] // 2
    row = jnp.sum(value, axis=0, keepdims=True)
    return row[:, :half] + row[:, half:]


def kernel(
    sizes,
    left_dims_hbm, right_dims_hbm, psi_hbm, left_hbm, right_hbm,
    state_hbm, folded_hbm,
    left_dims, right_dims, psi, left, right,
    sl0, sr0, sl1, sr1, pack_l, pack_r, got_l, got_r, got_psi,
    vec, cor, img_a, img_b, acc, acc_b, core_a, half_a, part_a,
    nacc, mats, core_m, half_m, part_m, part_n, hop_out, hop_in, folded,
    sums, ns_mine, cor_got, tag_out, tag_in,
    in_sem, pack_send, pack_recv, one_send, one_recv, sum_core, sum_core_in, sum_x, sum_x_in,
    all_core, all_core_in, all_x, all_x_in, s_send, s_recv, chain,
):
    ns, zs, tg, terms, width = sizes
    ys, xs = ns // zs, tg // CORES
    half = width // 2
    me, lane = lax.axis_index("sec"), lax.axis_index("term")
    x, c = lax.div(lane, CORES), lax.rem(lane, CORES)
    y, z = lax.div(me, zs), lax.rem(me, zs)
    up, down = lax.rem(me + 1, ns), lax.rem(me + ns - 1, ns)
    partner = lane + 1 - 2 * c
    far_first = sorted(range(1, xs), key=lambda d: -min(d, xs - d))
    order = [lax.rem(x + d, xs) for d in far_first] + [x]

    def send(src, dst, ssem, rsem, sec, term):
        return pltpu.make_async_remote_copy(
            src_ref=src, dst_ref=dst, send_sem=ssem, recv_sem=rsem,
            device_id=(sec, term), device_id_type=MESH,
        )

    barrier = pltpu.get_barrier_semaphore()
    groups = [
        [((me, lax.rem(lane + d, tg)), lax.rem(lane + d, tg)) for d in range(1, tg)],
        [((y * zs + lax.rem(z + d, zs), lane), lax.rem(z + d, zs)) for d in range(1, zs)],
        [((lax.rem(y + d, ys) * zs + z, lane), lax.rem(y + d, ys)) for d in range(1, ys)],
    ]
    places = [lane, z, y]
    rings = [
        [(y * zs + lax.rem(z + 1, zs), lane), (y * zs + lax.rem(z + zs - 1, zs), lane)],
        [(lax.rem(y + 1, ys) * zs + z, lane), (lax.rem(y + ys - 1, ys) * zs + z, lane)],
    ]
    reach = [zs // 2 - 1, ys // 2 - 1]
    greeted = [peer for peer, _ in groups[0]] + rings[0] + rings[1] + [(up, lane), (down, lane)]
    def vouch(turn):
        for axis in range(2):
            if turn < reach[axis]:
                for side, peer in enumerate(rings[axis]):
                    pl.semaphore_signal(
                        chain.at[axis, turn, side], inc=1, device_id=peer, device_id_type=MESH
                    )

    def vouched(turn):
        for axis in range(2):
            if turn < reach[axis]:
                for side in range(2):
                    pl.semaphore_wait(chain.at[axis, turn, side], 1)

    def load(src, dst, slot):
        return pltpu.make_async_copy(src, dst, in_sem.at[slot])

    rest = pl.ds(1, terms - 1)
    loads = [
        load(left_hbm.at[0], left.at[0], 0),
        load(right_hbm.at[0], right.at[0], 1),
        load(psi_hbm, psi, 2),
        load(left_hbm.at[rest], left.at[rest], 3),
        load(right_hbm.at[rest], right.at[rest], 4),
        load(left_dims_hbm, left_dims, 5),
        load(right_dims_hbm, right_dims, 6),
    ]
    for copy in loads[:2]:
        copy.start()
    for peer in greeted:
        pl.semaphore_signal(barrier, inc=1, device_id=peer, device_id_type=MESH)
    for copy in loads[2:]:
        copy.start()

    row_h = lax.broadcasted_iota(jnp.int32, (half, half), 0)
    col_h = lax.broadcasted_iota(jnp.int32, (half, half), 1)

    def prepare(t, raw, sym, pack):
        wide = raw[t].astype(F32)
        whole = (wide + wide.T).astype(BF16)
        sym[t] = whole
        again = whole.astype(F32)
        low, high = again[:half, :half], again[half:, half:]
        pack[t, :half] = whole[:half, half:]
        pack[t, half:width] = jnp.where(row_h <= col_h, low, high).astype(BF16)
        diag = jnp.sum(jnp.where(row_h == col_h, high, 0.0), axis=0, keepdims=True)
        pack[t, width:] = jnp.broadcast_to(diag, (8, half)).astype(BF16)

    def restore(t, pack, sym):
        corner = pack[t, :half].astype(F32)
        mixed = pack[t, half:width].astype(F32)
        diag = pack[t, width:].astype(F32)[0:1]
        turned = mixed.T
        sym[t, :half, :half] = jnp.where(row_h <= col_h, mixed, turned).astype(BF16)
        sym[t, :half, half:] = pack[t, :half]
        sym[t, half:, :half] = corner.T.astype(BF16)
        lower = jnp.where(row_h == col_h, jnp.broadcast_to(diag, (half, half)), turned)
        sym[t, half:, half:] = jnp.where(row_h > col_h, mixed, lower).astype(BF16)

    def ops_copies(t):
        return (
            send(pack_l.at[t], got_l.at[t], pack_send.at[0], pack_recv.at[0, t], down, lane),
            send(pack_r.at[t], got_r.at[t], pack_send.at[1], pack_recv.at[1, t], up, lane),
        )

    def prepare_both(t):
        prepare(t, left, sl0, pack_l)
        prepare(t, right, sr0, pack_r)

    waits = []

    def start(*copies):
        for copy in copies:
            copy.start()

    def start_one(*copies):
        start(*copies)
        waits.extend(copies)

    def rows(ref, first, count):
        return ref.at[..., pl.ds(pl.multiple_of(first, count), count), :]

    def top(ref, count):
        return ref.at[..., pl.ds(0, count), :]

    def gather_start(ref, slot):
        hr, qr = ref.shape[-2] // 2, ref.shape[-2] // 2 // xs
        own = rows(ref, c * hr + x * qr, qr)
        for i in range(xs - 1):
            start(send(own, own, all_x.at[slot], all_x_in.at[slot, x], me, order[i] * CORES + c))
        start(send(own, own, all_core.at[slot], all_core_in.at[slot], me, partner))
        most = top(ref, (xs - 1) * qr)
        waits.append(send(most, most, all_x.at[slot], all_x_in.at[slot, x], me, order[0] * CORES + c))
        most = top(ref, hr)
        waits.append(send(most, most, all_core.at[slot], all_core_in.at[slot], me, partner))

    def gather_pass(ref, slot):
        hr, qr = ref.shape[-2] // 2, ref.shape[-2] // 2 // xs
        for i in reversed(range(xs - 1)):
            piece = rows(ref, c * hr + order[i] * qr, qr)
            send(
                piece, piece, all_x.at[slot], all_x_in.at[slot, order[i]], me, order[i] * CORES + c
            ).wait_recv()
            start(send(piece, piece, all_core.at[slot], all_core_in.at[slot], me, partner))

    def gather_end(ref, slot):
        hr = ref.shape[-2] // 2
        piece = rows(ref, (1 - c) * hr, hr)
        send(piece, piece, all_core.at[slot], all_core_in.at[slot], me, partner).wait_recv()

    def core_copies(buf, core, slot):
        hr, qr = core.shape[-2], core.shape[-2] // xs
        return [
            send(
                rows(buf, (1 - c) * hr + xi * qr, qr), rows(core, xi * qr, qr),
                sum_core.at[slot], sum_core_in.at[slot, i], me, partner,
            )
            for i, xi in enumerate(order)
        ]

    def scatter_start(buf, core, slot):
        start(*core_copies(buf, core, slot))
        waits.append(send(core, core, sum_core.at[slot], sum_core_in.at[slot, 0], me, partner))

    def scatter_pass(buf, core, halved, part, slot):
        hr, qr = core.shape[-2], core.shape[-2] // xs
        copies = core_copies(buf, core, slot)
        late = None
        for i, xi in enumerate(order):
            copies[i].wait_recv()
            mine = rows(buf, c * hr + xi * qr, qr)[...] + rows(core, xi * qr, qr)[...]
            if i < xs - 1:
                piece = rows(halved, xi * qr, qr)
                piece[...] = mine
                now = send(piece, part.at[x], sum_x.at[slot], sum_x_in.at[slot], me, xi * CORES + c)
            else:
                part[x] = mine
                now = None
            if late is not None:
                start(late)
            late = now
        most = top(halved, (xs - 1) * qr)
        waits.append(send(most, most, sum_x.at[slot], sum_x_in.at[slot], me, order[0] * CORES + c))

    def scatter_end(part, slot):
        most = part.at[pl.ds(0, xs - 1)]
        send(most, most, sum_x.at[slot], sum_x_in.at[slot], me, order[0] * CORES + c).wait_recv()
        total = part[0]
        for i in range(1, xs):
            total = total + part[i]
        return total

    def scalar_all(rnd, stage):
        count = len(groups[stage])
        most = sums.at[rnd, stage, pl.ds(0, count)]
        index = rnd if rnd < 2 else 2 + stage
        return send(most, most, s_send.at[index], s_recv.at[index], *groups[stage][0][0])

    def scalar_start(rnd, stage, value):
        sums[rnd, stage, places[stage]] = value
        own = sums.at[rnd, stage, places[stage]]
        index = rnd if rnd < 2 else 2 + stage
        for peer, _ in groups[stage]:
            start(send(own, own, s_send.at[index], s_recv.at[index], *peer))
        waits.append(scalar_all(rnd, stage))

    def scalar_wait(rnd, stage):
        scalar_all(rnd, stage).wait_recv()
        total = sums[rnd, stage, 0]
        for i in range(1, len(groups[stage]) + 1):
            total = total + sums[rnd, stage, i]
        return total

    one_hot = lax.broadcasted_iota(jnp.int32, (8, half), 0) == lax.broadcasted_iota(jnp.int32, (8, half), 1)

    def row_of(values):
        values = jnp.concatenate(values + [jnp.zeros((8 - len(values), half), F32)], axis=0)
        full = jnp.broadcast_to(jnp.sum(values, axis=1, keepdims=True), (8, half))
        return jnp.sum(jnp.where(one_hot, full, 0.0), axis=0, keepdims=True)

    def column_of(row):
        return jnp.sum(jnp.where(one_hot, jnp.broadcast_to(row, (8, half)), 0.0), axis=1, keepdims=True)

    loads[0].wait()
    loads[1].wait()
    prepare_both(0)
    loads[2].wait()
    pl.semaphore_wait(barrier, len(greeted))
    vouch(0)
    psi_rows = width // tg
    psi_piece = rows(got_psi, c * half + x * psi_rows, psi_rows)
    psi_copy = send(
        rows(psi.at[2], c * half + x * psi_rows, psi_rows), psi_piece,
        one_send.at[0], one_recv.at[0], up, lane,
    )
    start_one(psi_copy)
    for copy in loads[3:]:
        copy.wait()

    @pl.loop(1, terms)
    def _(t):
        prepare_both(t)
        for copy in ops_copies(t - 1):
            copy.start()

    rows_own = left_dims[me]
    rows_next = jnp.where(me + 1 < ns, left_dims[up], 0)
    cols_own = right_dims[me]
    cols_last = jnp.where(me >= 1, right_dims[down], 0)
    live_rows = [rows_own, rows_next, rows_next]
    live_cols = [cols_own, cols_own, cols_last]

    def mask_of(k, first_row, count):
        row = lax.broadcasted_iota(jnp.int32, (count, width), 0) + first_row
        col = lax.broadcasted_iota(jnp.int32, (count, width), 1)
        return (row < live_rows[k]) & (col < live_cols[k])

    for k in range(2):
        vec[k] = jnp.where(mask_of(k, 0, width), psi[k].astype(F32), 0.0).astype(BF16)
    for copy in ops_copies(terms - 1):
        copy.start()

    scale, each = NOISE_WEIGHT / (terms * tg), 1.0 / tg
    quarter = half // xs
    own_row = pl.multiple_of(c * half + x * quarter, quarter)
    teams = [(0,), (1, 2)]

    def part_own(t, blocks, images, total):
        image = dot(sl0[t], blocks[0]).astype(BF16)
        images[t, 0] = image
        total[0] += dot(image, sr0[t])

    def part_one(t, blocks, images, total):
        image = dot(sl1[t], blocks[1]).astype(BF16)
        images[t, 1] = image
        total[1] += dot(image, sr0[t])

    def part_two(t, blocks, images, total):
        image = dot(sl1[t], blocks[2]).astype(BF16)
        images[t, 2] = image
        total[2] += dot(image, sr1[t])

    def grow(slot, team, one, two, t):
        for k in teams[team]:
            nacc[team, slot] += dot_t(one[t, k], two[t, k])

    def put_folded(slot, team, full):
        mats[team, slot, :half] = full[:half, :half]
        mats[team, slot, half:width] = full[:half, half:]
        mats[team, slot, width:] = full[half:, half:]

    def own_part(team, one, two):
        total = dot_t(one[teams[team][0]], two[teams[team][0]])
        for k in teams[team][1:]:
            total = total + dot_t(one[k], two[k])
        return each * total

    def put_plain(slot, team, one):
        put_folded(slot, team, scale * nacc[team, slot] + own_part(team, one, one))

    def put_cross(slot, team, one, two):
        cross = scale * nacc[team, slot] + own_part(team, one, two)
        put_folded(slot, team, cross + cross.T)

    def norms(team):
        h_row = a_row = jnp.zeros((1, half), F32)
        for k in teams[team]:
            wide = vec[k].astype(F32)
            h_row = h_row + fold(wide * acc[k])
            a_row = a_row + fold(wide * wide)
        return h_row, a_row

    def level_of(rnd):
        total = column_of(scalar_wait(rnd, 0))
        h_here, a_here = total[0:1], total[1:2] * each
        some = a_here > 0.0
        return jnp.where(some, h_here / jnp.where(some, a_here, 1.0), 0.0)

    def correct(k, level, shard):
        held = vec[k, pl.ds(own_row, quarter), :].astype(F32)
        inside_k = jnp.where(mask_of(k, own_row, quarter), shard[0], 0.0)
        cor[k, pl.ds(own_row, quarter), :] = (inside_k - level * held).astype(BF16)

    acc_of = [acc.at[pl.ds(k, 1)] for k in range(3)]
    core_of = [core_a.at[pl.ds(k, 1)] for k in range(3)]
    half_of = [half_a.at[pl.ds(k, 1)] for k in range(3)]
    part_of = [part_a.at[k] for k in range(3)]
    cor_of = [cor.at[pl.ds(k, 1)] for k in range(3)]

    def arrive(t):
        for copy in ops_copies(t):
            copy.wait_recv()
        restore(t, got_l, sl1)
        restore(t, got_r, sr1)

    acc[...] = jnp.zeros_like(acc)
    acc_b[...] = jnp.zeros_like(acc_b)
    nacc[...] = jnp.zeros_like(nacc)

    @pl.loop(0, terms, unroll=4)
    def _(t):
        part_own(t, vec, img_a, acc)

    scatter_start(acc_of[0], core_of[0], 0)
    h_zero, a_zero = norms(0)
    scalar_start(0, 0, row_of([h_zero, a_zero]))
    psi_copy.wait_recv()
    gather_start(got_psi, 0)
    scatter_pass(acc_of[0], core_of[0], half_of[0], part_of[0], 0)

    @pl.loop(0, terms, unroll=4)
    def _(t):
        grow(0, 0, img_a, img_a, t)

    early = terms // 4
    for t in range(early):
        arrive(t)
        part_one(t, vec, img_a, acc)
    vouched(0)
    vouch(1)
    gather_pass(got_psi, 0)
    level_zero = level_of(0)
    shard = scatter_end(part_of[0], 0)
    correct(0, level_zero, shard)
    gather_start(cor_of[0], 1)
    gather_end(got_psi, 0)
    vec[2] = jnp.where(mask_of(2, 0, width), got_psi[...].astype(F32), 0.0).astype(BF16)
    for t in range(early):
        part_two(t, vec, img_a, acc)
    middle = terms // 2
    for t in range(early, middle):
        arrive(t)
        part_one(t, vec, img_a, acc)
        part_two(t, vec, img_a, acc)
    vouched(1)
    vouch(2)
    gather_pass(cor_of[0], 1)
    for t in range(middle, middle + 1):
        arrive(t)
        part_one(t, vec, img_a, acc)
        part_two(t, vec, img_a, acc)
    gather_end(cor_of[0], 1)

    @pl.loop(0, terms, unroll=4)
    def _(t):
        part_own(t, cor, img_b, acc_b)

    for turn in range(2, max(reach)):
        vouched(turn)
        vouch(turn + 1)
    for t in range(middle + 1, terms):
        arrive(t)
        part_one(t, vec, img_a, acc)
        part_two(t, vec, img_a, acc)
    scatter_start(acc_of[1], core_of[1], 1)
    scatter_start(acc_of[2], core_of[2], 6)
    h_near, a_near = norms(1)
    scalar_start(1, 0, row_of([h_near, a_near]))

    @pl.loop(0, terms, unroll=4)
    def _(t):
        grow(1, 0, img_b, img_b, t)

    scatter_pass(acc_of[1], core_of[1], half_of[1], part_of[1], 1)
    scatter_pass(acc_of[2], core_of[2], half_of[2], part_of[2], 6)

    @pl.loop(0, terms, unroll=4)
    def _(t):
        grow(2, 0, img_a, img_b, t)

    put_plain(0, 0, vec)
    put_plain(1, 0, cor)
    put_cross(2, 0, vec, cor)
    scatter_start(mats.at[0], core_m.at[0], 2)
    level_near = level_of(1)
    shard = scatter_end(part_of[1], 1)
    correct(1, level_near, shard)
    gather_start(cor_of[1], 2)
    shard = scatter_end(part_of[2], 6)
    correct(2, level_near, shard)
    gather_start(cor_of[2], 3)

    @pl.loop(0, terms, unroll=4)
    def _(t):
        grow(0, 1, img_a, img_a, t)

    put_plain(0, 1, vec)
    scatter_start(mats.at[1, 0], core_m.at[1, 0], 3)
    gather_pass(cor_of[1], 2)
    gather_end(cor_of[1], 2)

    @pl.loop(0, middle, unroll=True)
    def _(t):
        part_one(t, cor, img_b, acc_b)

    gather_pass(cor_of[2], 3)

    @pl.loop(middle, terms, unroll=True)
    def _(t):
        part_one(t, cor, img_b, acc_b)

    gather_end(cor_of[2], 3)
    tag_out[...] = jnp.broadcast_to(level_near, (8, half))
    scatter_pass(mats.at[0], core_m.at[0], half_m.at[0], part_m, 2)

    @pl.loop(0, terms, unroll=4)
    def _(t):
        part_two(t, cor, img_b, acc_b)

    levels = [level_zero, level_near]
    sides = [(h_zero, a_zero), (h_near, a_near)]
    gathered = [jnp.zeros((1, half), F32)] * 6
    for team in range(2):
        level, (h_row, a_row) = levels[team], sides[team]
        vc = cc = vhc = chc = jnp.zeros((1, half), F32)
        for k in teams[team]:
            wide, corr = vec[k].astype(F32), cor[k].astype(F32)
            summed = acc_b[k]
            vc = vc + fold(wide * corr)
            cc = cc + fold(corr * corr)
            vhc = vhc + fold(wide * summed)
            chc = chc + fold(corr * summed)
        here = [
            a_row * each,
            h_row,
            (vc + level * a_row) * each,
            (cc + level * (2.0 * vc + level * a_row)) * each,
            vhc + level * h_row,
            chc + level * (2.0 * vhc + level * h_row),
        ]
        gathered = [one + two for one, two in zip(gathered, here)]
    scalar_start(2, 1, row_of(gathered))
    scatter_pass(mats.at[1, 0], core_m.at[1, 0], half_m.at[1, 0], part_n.at[0], 3)

    @pl.loop(0, terms, unroll=4)
    def _(t):
        grow(1, 1, img_b, img_b, t)

    put_plain(1, 1, cor)
    scatter_start(mats.at[1, 1], core_m.at[1, 1], 4)

    @pl.loop(0, terms, unroll=4)
    def _(t):
        grow(2, 1, img_a, img_b, t)

    put_cross(2, 1, vec, cor)
    scatter_start(mats.at[1, 2], core_m.at[1, 2], 5)
    scatter_pass(mats.at[1, 1], core_m.at[1, 1], half_m.at[1, 1], part_n.at[1], 4)
    scalar_start(2, 2, scalar_wait(2, 1))
    to_owner = [
        send(cor.at[2], cor_got, one_send.at[2], one_recv.at[2], down, lane),
        send(tag_out, tag_in, one_send.at[3], one_recv.at[3], down, lane),
    ]
    start_one(*to_owner)
    scatter_pass(mats.at[1, 2], core_m.at[1, 2], half_m.at[1, 2], part_n.at[2], 5)
    scalar_start(2, 0, scalar_wait(2, 2))
    stay = scatter_end(part_m, 2)
    count = stay.shape[1]
    for q in range(3):
        hop_out[q * count:(q + 1) * count] = scatter_end(part_n.at[q], 3 + q)
    hop_out[3 * count:] = jnp.broadcast_to(level_near, (8, half))
    hop = send(hop_out, hop_in, one_send.at[1], one_recv.at[1], up, lane)
    start_one(hop)
    whole = column_of(scalar_wait(2, 0))
    a11, h11, v_u, u_u, v_hu, u_hu = [whole[q:q + 1] for q in range(6)]
    mean = h11 / a11
    a12 = v_u - mean * a11
    a22 = u_u - mean * (2.0 * v_u - mean * a11)
    h12 = v_hu - mean * h11
    h22 = u_hu - mean * (2.0 * v_hu - mean * h11)
    quad_a = a11 * a22 - a12 * a12
    quad_b = h11 * a22 + h22 * a11 - 2.0 * h12 * a12
    quad_c = h11 * h22 - h12 * h12
    lowest = (quad_b - jnp.sqrt(jnp.maximum(quad_b * quad_b - 4.0 * quad_a * quad_c, 0.0))) / (
        2.0 * quad_a
    )
    ratio = (lowest * a11 - h11) / (h12 - lowest * a12)
    first_coef = lax.rsqrt(a11 + 2.0 * ratio * a12 + ratio * ratio * a22)
    second_coef = ratio * first_coef

    def weigh(coef, parts):
        return coef * coef * parts[0] + coef * second_coef * parts[2] + second_coef * second_coef * parts[1]

    coefs = [first_coef + second_coef * (level - mean) for level in levels]
    stay = weigh(coefs[0], [stay[q] for q in range(3)])
    hop.wait_recv()
    coef_last = first_coef + second_coef * (hop_in[3 * count:3 * count + 1, 0:1] - mean)
    come = weigh(coef_last, [hop_in[q * count:(q + 1) * count] for q in range(3)])
    piled = folded.at[pl.ds(0, 3 * half)]
    rows(piled, (c * xs + x) * count, count)[...] = stay + come
    gather_start(piled, 4)
    for copy in to_owner:
        copy.wait_recv()
    coefs.append(first_coef + second_coef * (tag_in[0:1, 0:1] - mean))
    rows_last = jnp.where(me + 2 < ns, left_dims[lax.rem(me + 2, ns)], 0)
    row = lax.broadcasted_iota(jnp.int32, (width, width), 0)
    col = lax.broadcasted_iota(jnp.int32, (width, width), 1)
    last = jnp.where((row < rows_last) & (col < cols_own), psi[2].astype(F32), 0.0)
    pairs = [(vec[k].astype(F32), cor[k].astype(F32)) for k in range(2)] + [(last, cor_got[...].astype(F32))]
    for k, (wide, corr) in enumerate(pairs):
        ns_mine[k] = (coefs[k] * wide + second_coef * corr).astype(BF16)
    tail = lax.broadcasted_iota(jnp.int32, (8, half), 0)
    live = jnp.broadcast_to(rows_own, (8, half)).astype(F32)
    folded[3 * half:] = jnp.where(tail == 0, live, lowest)
    state_copy = load(ns_mine, state_hbm, 7)
    state_copy.start()
    gather_pass(piled, 4)
    gather_end(piled, 4)
    folded_copy = load(folded, folded_hbm, 8)
    folded_copy.start()
    send(pack_l, got_l, pack_send.at[0], pack_recv.at[0, 0], down, lane).wait_send()
    send(pack_r, got_r, pack_send.at[1], pack_recv.at[1, 0], up, lane).wait_send()
    for copy in waits:
        copy.wait_send()
    state_copy.wait()
    folded_copy.wait()


def sign_kernel(half, folded, state_hbm, new_state_hbm, kept, energy, state, sem):
    width = 2 * half
    into = pltpu.make_async_copy(state_hbm, state, sem.at[0])
    into.start()
    row = lax.broadcasted_iota(jnp.int32, (width, width), 0)
    col = lax.broadcasted_iota(jnp.int32, (width, width), 1)
    identity = jnp.where(row == col, 1.0, 0.0).astype(F32)
    live = folded[3 * half:3 * half + 1, 0:1]
    energy[...] = folded[3 * half + 1:3 * half + 2, 0:1]
    corner = folded[half:width]
    density = jnp.concatenate([
        jnp.concatenate([folded[:half], corner], axis=1),
        jnp.concatenate([corner.T, folded[width:3 * half]], axis=1),
    ], axis=0)
    inside = (row.astype(F32) < live) & (col.astype(F32) < live)
    density = jnp.where(inside, density, 0.0)
    trace = jnp.sum(jnp.sum(density * identity, axis=0, keepdims=True), axis=1, keepdims=True)
    shifted = density - (trace / live) * identity
    square = jnp.sum(jnp.sum(shifted * shifted, axis=0, keepdims=True), axis=1, keepdims=True)
    kept[...] = shifted / jnp.sqrt(square)
    out = pltpu.make_async_copy(state, new_state_hbm, sem.at[1])

    def step():
        current = kept[...]
        high, low = halves(current)
        stacked = jnp.concatenate([high, low, high], axis=0)
        for first in range(0, width, half):
            block = slice(first, first + half)
            squared = dot(beside(high[block], low[block]), stacked)
            cubed = dot(beside(*halves(squared)), stacked)
            kept[block] = 1.5 * current[block] - 0.5 * cubed

    pl.loop(0, SIGN_STEPS // 2)(lambda _: step())
    into.wait()
    out.start()
    pl.loop(SIGN_STEPS // 2, SIGN_STEPS)(lambda _: step())
    kept[...] = 0.5 * (identity + kept[...])
    out.wait()


def per_device(zs, ns, tg, psi, left_ops, right_ops, left_dims, right_dims):
    terms, width = left_ops.shape[0], left_ops.shape[-1]
    half, xs = width // 2, tg // CORES
    quarter, ys = half // xs, ns // zs
    tall = 3 * half
    share = tall // 2 // xs
    most = max(tg, zs, ys)
    vmem, hbm = pl.BlockSpec(memory_space=pltpu.VMEM), pl.BlockSpec(memory_space=pltpu.HBM)
    dma = pltpu.SemaphoreType.DMA
    state, folded = pl.pallas_call(
        functools.partial(kernel, (ns, zs, tg, terms, width)),
        out_shape=(
            jax.ShapeDtypeStruct((3, width, width), BF16),
            jax.ShapeDtypeStruct((tall + 8, half), F32),
        ),
        in_specs=[hbm] * 5,
        out_specs=(hbm, hbm),
        scratch_shapes=[pltpu.SMEM((ns,), jnp.int32)] * 2
        + [pltpu.VMEM((3, width, width), BF16)]
        + [pltpu.VMEM((terms, width, width), BF16)] * 6
        + [pltpu.VMEM((terms, width + 8, half), BF16)] * 4
        + [pltpu.VMEM((width, width), BF16)]
        + [pltpu.VMEM((3, width, width), BF16)] * 2
        + [pltpu.VMEM((terms, 3, width, width), BF16)] * 2
        + [pltpu.VMEM((3, width, width), F32)] * 2
        + [pltpu.VMEM((3, half, width), F32)] * 2
        + [pltpu.VMEM((3, xs, 1, quarter, width), F32)]
        + [pltpu.VMEM((2, 3, width, width), F32)]
        + [pltpu.VMEM((2, 3, tall, half), F32)]
        + [pltpu.VMEM((2, 3, tall // 2, half), F32)] * 2
        + [pltpu.VMEM((xs, 3, share, half), F32)]
        + [pltpu.VMEM((3, xs, share, half), F32)]
        + [pltpu.VMEM((3 * share + 8, half), F32)] * 2
        + [pltpu.VMEM((tall + 8, half), F32)]
        + [pltpu.VMEM((3, 3, most, 1, half), F32)]
        + [pltpu.VMEM((3, width, width), BF16), pltpu.VMEM((width, width), BF16)]
        + [pltpu.VMEM((8, half), F32)] * 2
        + [dma((9,)), dma((2,)), dma((2, terms)), dma((4,)), dma((4,))]
        + [dma((7,)), dma((7, xs)), dma((7,)), dma((7,)), dma((5,)), dma((5,)), dma((5,)), dma((5, xs))]
        + [dma((5,))] * 2
        + [pltpu.SemaphoreType.REGULAR((2, max(zs // 2, ys // 2, 2) - 1, 2))],
        compiler_params=pltpu.CompilerParams(
            collective_id=0, has_side_effects=True, vmem_limit_bytes=67043328
        ),
    )(left_dims, right_dims, psi[0], left_ops[:, 0], right_ops[:, 0])
    new_state, kept, energy = pl.pallas_call(
        functools.partial(sign_kernel, half),
        out_shape=(
            jax.ShapeDtypeStruct((3, width, width), BF16),
            jax.ShapeDtypeStruct((width, width), F32),
            jax.ShapeDtypeStruct((1, 1), F32),
        ),
        in_specs=[vmem, hbm],
        out_specs=(hbm, vmem, vmem),
        scratch_shapes=[pltpu.VMEM((3, width, width), BF16), dma((2,))],
    )(folded, state)
    return new_state[None], kept[None], energy[0, 0]


def solution(mesh):
    ns, tg = mesh.shape["sec"], mesh.shape["term"]
    zs = ZSIZE if ns % ZSIZE == 0 and ns > ZSIZE else 2
    in_specs = (
        P("sec", None, None, None),
        P("term", "sec", None, None),
        P("term", "sec", None, None),
        P(),
        P(),
    )
    out_specs = (P("sec", None, None, None), P("sec", None, None), P())
    return jax.shard_map(
        functools.partial(per_device, zs, ns, tg),
        mesh=mesh, in_specs=in_specs, out_specs=out_specs, check_vma=False,
    )
```

```python
import functools

import jax
import jax.numpy as jnp
from jax import lax
from jax.experimental import pallas as pl
from jax.experimental.pallas import tpu as pltpu
from jax.sharding import PartitionSpec as P

SIGN_STEPS = 6
ZSIZE = 8
CORES = 2
NOISE_WEIGHT = 0.5
MESH = pl.DeviceIdType.MESH
F32 = jnp.float32
BF16 = jnp.bfloat16


def dot(a, b):
    return jnp.dot(a, b, preferred_element_type=F32)


def dot_t(a, b):
    return lax.dot_general(a, b, (((1,), (1,)), ((), ())), preferred_element_type=F32)


def halves(value):
    high = value.astype(BF16)
    return high, (value - high.astype(F32)).astype(BF16)


def beside(high, low):
    return jnp.concatenate([high, high, low], axis=1)


def fold(value):
    half = value.shape[1] // 2
    row = jnp.sum(value, axis=0, keepdims=True)
    return row[:, :half] + row[:, half:]


def kernel(
    sizes,
    left_dims_hbm, right_dims_hbm, psi_hbm, left_hbm, right_hbm,
    state_hbm, folded_hbm,
    left_dims, right_dims, psi, left, right,
    sl0, sr0, sl1, sr1, pack_l, pack_r, got_l, got_r, got_psi,
    vec, cor, img_a, img_b, acc, acc_b, core_a, half_a, part_a,
    nacc, mats, core_m, half_m, part_m, part_n, hop_out, hop_in, folded,
    sums, ns_mine, cor_got, tag_out, tag_in,
    in_sem, pack_send, pack_recv, one_send, one_recv, sum_core, sum_core_in, sum_x, sum_x_in,
    all_core, all_core_in, all_x, all_x_in, s_send, s_recv, chain,
):
    ns, zs, tg, terms, width = sizes
    ys, xs = ns // zs, tg // CORES
    half = width // 2
    me, lane = lax.axis_index("sec"), lax.axis_index("term")
    x, c = lax.div(lane, CORES), lax.rem(lane, CORES)
    y, z = lax.div(me, zs), lax.rem(me, zs)
    up, down = lax.rem(me + 1, ns), lax.rem(me + ns - 1, ns)
    partner = lane + 1 - 2 * c
    far_first = sorted(range(1, xs), key=lambda d: -min(d, xs - d))
    order = [lax.rem(x + d, xs) for d in far_first] + [x]

    def send(src, dst, ssem, rsem, sec, term):
        return pltpu.make_async_remote_copy(
            src_ref=src, dst_ref=dst, send_sem=ssem, recv_sem=rsem,
            device_id=(sec, term), device_id_type=MESH,
        )

    barrier = pltpu.get_barrier_semaphore()
    groups = [
        [((me, lax.rem(lane + d, tg)), lax.rem(lane + d, tg)) for d in range(1, tg)],
        [((y * zs + lax.rem(z + d, zs), lane), lax.rem(z + d, zs)) for d in range(1, zs)],
        [((lax.rem(y + d, ys) * zs + z, lane), lax.rem(y + d, ys)) for d in range(1, ys)],
    ]
    places = [lane, z, y]
    rings = [
        [(y * zs + lax.rem(z + 1, zs), lane), (y * zs + lax.rem(z + zs - 1, zs), lane)],
        [(lax.rem(y + 1, ys) * zs + z, lane), (lax.rem(y + ys - 1, ys) * zs + z, lane)],
    ]
    reach = [zs // 2 - 1, ys // 2 - 1]
    greeted = [peer for peer, _ in groups[0]] + rings[0] + rings[1] + [(up, lane), (down, lane)]
    def vouch(turn):
        for axis in range(2):
            if turn < reach[axis]:
                for side, peer in enumerate(rings[axis]):
                    pl.semaphore_signal(
                        chain.at[axis, turn, side], inc=1, device_id=peer, device_id_type=MESH
                    )

    def vouched(turn):
        for axis in range(2):
            if turn < reach[axis]:
                for side in range(2):
                    pl.semaphore_wait(chain.at[axis, turn, side], 1)

    def load(src, dst, slot):
        return pltpu.make_async_copy(src, dst, in_sem.at[slot])

    rest = pl.ds(1, terms - 1)
    loads = [
        load(left_hbm.at[0], left.at[0], 0),
        load(right_hbm.at[0], right.at[0], 1),
        load(psi_hbm, psi, 2),
        load(left_hbm.at[rest], left.at[rest], 3),
        load(right_hbm.at[rest], right.at[rest], 4),
        load(left_dims_hbm, left_dims, 5),
        load(right_dims_hbm, right_dims, 6),
    ]
    for copy in loads[:2]:
        copy.start()
    for peer in greeted:
        pl.semaphore_signal(barrier, inc=1, device_id=peer, device_id_type=MESH)
    for copy in loads[2:]:
        copy.start()

    row_h = lax.broadcasted_iota(jnp.int32, (half, half), 0)
    col_h = lax.broadcasted_iota(jnp.int32, (half, half), 1)

    def prepare(t, raw, sym, pack):
        wide = raw[t].astype(F32)
        whole = (wide + wide.T).astype(BF16)
        sym[t] = whole
        again = whole.astype(F32)
        low, high = again[:half, :half], again[half:, half:]
        pack[t, :half] = whole[:half, half:]
        pack[t, half:width] = jnp.where(row_h <= col_h, low, high).astype(BF16)
        diag = jnp.sum(jnp.where(row_h == col_h, high, 0.0), axis=0, keepdims=True)
        pack[t, width:] = jnp.broadcast_to(diag, (8, half)).astype(BF16)

    def restore(t, pack, sym):
        corner = pack[t, :half].astype(F32)
        mixed = pack[t, half:width].astype(F32)
        diag = pack[t, width:].astype(F32)[0:1]
        turned = mixed.T
        sym[t, :half, :half] = jnp.where(row_h <= col_h, mixed, turned).astype(BF16)
        sym[t, :half, half:] = pack[t, :half]
        sym[t, half:, :half] = corner.T.astype(BF16)
        lower = jnp.where(row_h == col_h, jnp.broadcast_to(diag, (half, half)), turned)
        sym[t, half:, half:] = jnp.where(row_h > col_h, mixed, lower).astype(BF16)

    def ops_copies(t):
        return (
            send(pack_l.at[t], got_l.at[t], pack_send.at[0], pack_recv.at[0, t], down, lane),
            send(pack_r.at[t], got_r.at[t], pack_send.at[1], pack_recv.at[1, t], up, lane),
        )

    def prepare_both(t):
        prepare(t, left, sl0, pack_l)
        prepare(t, right, sr0, pack_r)

    waits = []

    def start(*copies):
        for copy in copies:
            copy.start()

    def start_one(*copies):
        start(*copies)
        waits.extend(copies)

    def rows(ref, first, count):
        return ref.at[..., pl.ds(pl.multiple_of(first, count), count), :]

    def top(ref, count):
        return ref.at[..., pl.ds(0, count), :]

    def gather_start(ref, slot):
        hr, qr = ref.shape[-2] // 2, ref.shape[-2] // 2 // xs
        own = rows(ref, c * hr + x * qr, qr)
        for i in range(xs - 1):
            start(send(own, own, all_x.at[slot], all_x_in.at[slot, x], me, order[i] * CORES + c))
        start(send(own, own, all_core.at[slot], all_core_in.at[slot], me, partner))
        most = top(ref, (xs - 1) * qr)
        waits.append(send(most, most, all_x.at[slot], all_x_in.at[slot, x], me, order[0] * CORES + c))
        most = top(ref, hr)
        waits.append(send(most, most, all_core.at[slot], all_core_in.at[slot], me, partner))

    def gather_pass(ref, slot):
        hr, qr = ref.shape[-2] // 2, ref.shape[-2] // 2 // xs
        for i in reversed(range(xs - 1)):
            piece = rows(ref, c * hr + order[i] * qr, qr)
            send(
                piece, piece, all_x.at[slot], all_x_in.at[slot, order[i]], me, order[i] * CORES + c
            ).wait_recv()
            start(send(piece, piece, all_core.at[slot], all_core_in.at[slot], me, partner))

    def gather_end(ref, slot):
        hr = ref.shape[-2] // 2
        piece = rows(ref, (1 - c) * hr, hr)
        send(piece, piece, all_core.at[slot], all_core_in.at[slot], me, partner).wait_recv()

    def core_copies(buf, core, slot):
        hr, qr = core.shape[-2], core.shape[-2] // xs
        return [
            send(
                rows(buf, (1 - c) * hr + xi * qr, qr), rows(core, xi * qr, qr),
                sum_core.at[slot], sum_core_in.at[slot, i], me, partner,
            )
            for i, xi in enumerate(order)
        ]

    def scatter_start(buf, core, slot):
        start(*core_copies(buf, core, slot))
        waits.append(send(core, core, sum_core.at[slot], sum_core_in.at[slot, 0], me, partner))

    def scatter_pass(buf, core, halved, part, slot):
        hr, qr = core.shape[-2], core.shape[-2] // xs
        copies = core_copies(buf, core, slot)
        late = None
        for i, xi in enumerate(order):
            copies[i].wait_recv()
            mine = rows(buf, c * hr + xi * qr, qr)[...] + rows(core, xi * qr, qr)[...]
            if i < xs - 1:
                piece = rows(halved, xi * qr, qr)
                piece[...] = mine
                now = send(piece, part.at[x], sum_x.at[slot], sum_x_in.at[slot], me, xi * CORES + c)
            else:
                part[x] = mine
                now = None
            if late is not None:
                start(late)
            late = now
        most = top(halved, (xs - 1) * qr)
        waits.append(send(most, most, sum_x.at[slot], sum_x_in.at[slot], me, order[0] * CORES + c))

    def scatter_end(part, slot):
        most = part.at[pl.ds(0, xs - 1)]
        send(most, most, sum_x.at[slot], sum_x_in.at[slot], me, order[0] * CORES + c).wait_recv()
        total = part[0]
        for i in range(1, xs):
            total = total + part[i]
        return total

    def scalar_all(rnd, stage):
        count = len(groups[stage])
        most = sums.at[rnd, stage, pl.ds(0, count)]
        index = rnd if rnd < 2 else 2 + stage
        return send(most, most, s_send.at[index], s_recv.at[index], *groups[stage][0][0])

    def scalar_start(rnd, stage, value):
        sums[rnd, stage, places[stage]] = value
        own = sums.at[rnd, stage, places[stage]]
        index = rnd if rnd < 2 else 2 + stage
        for peer, _ in groups[stage]:
            start(send(own, own, s_send.at[index], s_recv.at[index], *peer))
        waits.append(scalar_all(rnd, stage))

    def scalar_wait(rnd, stage):
        scalar_all(rnd, stage).wait_recv()
        total = sums[rnd, stage, 0]
        for i in range(1, len(groups[stage]) + 1):
            total = total + sums[rnd, stage, i]
        return total

    one_hot = lax.broadcasted_iota(jnp.int32, (8, half), 0) == lax.broadcasted_iota(jnp.int32, (8, half), 1)

    def row_of(values):
        values = jnp.concatenate(values + [jnp.zeros((8 - len(values), half), F32)], axis=0)
        full = jnp.broadcast_to(jnp.sum(values, axis=1, keepdims=True), (8, half))
        return jnp.sum(jnp.where(one_hot, full, 0.0), axis=0, keepdims=True)

    def column_of(row):
        return jnp.sum(jnp.where(one_hot, jnp.broadcast_to(row, (8, half)), 0.0), axis=1, keepdims=True)

    loads[0].wait()
    loads[1].wait()
    prepare_both(0)
    loads[2].wait()
    pl.semaphore_wait(barrier, len(greeted))
    vouch(0)
    psi_rows = width // tg
    psi_piece = rows(got_psi, c * half + x * psi_rows, psi_rows)
    psi_copy = send(
        rows(psi.at[2], c * half + x * psi_rows, psi_rows), psi_piece,
        one_send.at[0], one_recv.at[0], up, lane,
    )
    start_one(psi_copy)
    for copy in loads[3:]:
        copy.wait()

    @pl.loop(1, terms)
    def _(t):
        prepare_both(t)
        for copy in ops_copies(t - 1):
            copy.start()

    rows_own = left_dims[me]
    rows_next = jnp.where(me + 1 < ns, left_dims[up], 0)
    cols_own = right_dims[me]
    cols_last = jnp.where(me >= 1, right_dims[down], 0)
    live_rows = [rows_own, rows_next, rows_next]
    live_cols = [cols_own, cols_own, cols_last]

    def mask_of(k, first_row, count):
        row = lax.broadcasted_iota(jnp.int32, (count, width), 0) + first_row
        col = lax.broadcasted_iota(jnp.int32, (count, width), 1)
        return (row < live_rows[k]) & (col < live_cols[k])

    for k in range(2):
        vec[k] = jnp.where(mask_of(k, 0, width), psi[k].astype(F32), 0.0).astype(BF16)
    for copy in ops_copies(terms - 1):
        copy.start()

    scale, each = NOISE_WEIGHT / (terms * tg), 1.0 / tg
    quarter = half // xs
    own_row = pl.multiple_of(c * half + x * quarter, quarter)
    teams = [(0,), (1, 2)]

    def part_own(t, blocks, images, total):
        image = dot(sl0[t], blocks[0]).astype(BF16)
        images[t, 0] = image
        total[0] += dot(image, sr0[t])

    def part_one(t, blocks, images, total):
        image = dot(sl1[t], blocks[1]).astype(BF16)
        images[t, 1] = image
        total[1] += dot(image, sr0[t])

    def part_two(t, blocks, images, total):
        image = dot(sl1[t], blocks[2]).astype(BF16)
        images[t, 2] = image
        total[2] += dot(image, sr1[t])

    def grow(slot, team, one, two, t):
        for k in teams[team]:
            nacc[team, slot] += dot_t(one[t, k], two[t, k])

    def put_folded(slot, team, full):
        mats[team, slot, :half] = full[:half, :half]
        mats[team, slot, half:width] = full[:half, half:]
        mats[team, slot, width:] = full[half:, half:]

    def own_part(team, one, two):
        total = dot_t(one[teams[team][0]], two[teams[team][0]])
        for k in teams[team][1:]:
            total = total + dot_t(one[k], two[k])
        return each * total

    def put_plain(slot, team, one):
        put_folded(slot, team, scale * nacc[team, slot] + own_part(team, one, one))

    def put_cross(slot, team, one, two):
        cross = scale * nacc[team, slot] + own_part(team, one, two)
        put_folded(slot, team, cross + cross.T)

    def norms(team):
        h_row = a_row = jnp.zeros((1, half), F32)
        for k in teams[team]:
            wide = vec[k].astype(F32)
            h_row = h_row + fold(wide * acc[k])
            a_row = a_row + fold(wide * wide)
        return h_row, a_row

    def level_of(rnd):
        total = column_of(scalar_wait(rnd, 0))
        h_here, a_here = total[0:1], total[1:2] * each
        some = a_here > 0.0
        return jnp.where(some, h_here / jnp.where(some, a_here, 1.0), 0.0)

    def correct(k, level, shard):
        held = vec[k, pl.ds(own_row, quarter), :].astype(F32)
        inside_k = jnp.where(mask_of(k, own_row, quarter), shard[0], 0.0)
        cor[k, pl.ds(own_row, quarter), :] = (inside_k - level * held).astype(BF16)

    acc_of = [acc.at[pl.ds(k, 1)] for k in range(3)]
    core_of = [core_a.at[pl.ds(k, 1)] for k in range(3)]
    half_of = [half_a.at[pl.ds(k, 1)] for k in range(3)]
    part_of = [part_a.at[k] for k in range(3)]
    cor_of = [cor.at[pl.ds(k, 1)] for k in range(3)]

    def arrive(t):
        for copy in ops_copies(t):
            copy.wait_recv()
        restore(t, got_l, sl1)
        restore(t, got_r, sr1)

    acc[...] = jnp.zeros_like(acc)
    acc_b[...] = jnp.zeros_like(acc_b)
    nacc[...] = jnp.zeros_like(nacc)

    @pl.loop(0, terms, unroll=True)
    def _(t):
        part_own(t, vec, img_a, acc)

    scatter_start(acc_of[0], core_of[0], 0)
    h_zero, a_zero = norms(0)
    scalar_start(0, 0, row_of([h_zero, a_zero]))
    psi_copy.wait_recv()
    gather_start(got_psi, 0)
    scatter_pass(acc_of[0], core_of[0], half_of[0], part_of[0], 0)

    @pl.loop(0, terms, unroll=4)
    def _(t):
        grow(0, 0, img_a, img_a, t)

    early = terms // 4
    for t in range(early):
        arrive(t)
        part_one(t, vec, img_a, acc)
    vouched(0)
    vouch(1)
    gather_pass(got_psi, 0)
    level_zero = level_of(0)
    shard = scatter_end(part_of[0], 0)
    correct(0, level_zero, shard)
    gather_start(cor_of[0], 1)
    gather_end(got_psi, 0)
    vec[2] = jnp.where(mask_of(2, 0, width), got_psi[...].astype(F32), 0.0).astype(BF16)
    for t in range(early):
        part_two(t, vec, img_a, acc)
    middle = terms // 2
    for t in range(early, middle):
        arrive(t)
        part_one(t, vec, img_a, acc)
        part_two(t, vec, img_a, acc)
    vouched(1)
    vouch(2)
    gather_pass(cor_of[0], 1)
    for t in range(middle, middle + 1):
        arrive(t)
        part_one(t, vec, img_a, acc)
        part_two(t, vec, img_a, acc)
    gather_end(cor_of[0], 1)

    @pl.loop(0, terms, unroll=4)
    def _(t):
        part_own(t, cor, img_b, acc_b)

    for turn in range(2, max(reach)):
        vouched(turn)
        vouch(turn + 1)
    for t in range(middle + 1, terms):
        arrive(t)
        part_one(t, vec, img_a, acc)
        part_two(t, vec, img_a, acc)
    scatter_start(acc_of[1], core_of[1], 1)
    scatter_start(acc_of[2], core_of[2], 6)
    h_near, a_near = norms(1)
    scalar_start(1, 0, row_of([h_near, a_near]))

    @pl.loop(0, terms, unroll=4)
    def _(t):
        grow(1, 0, img_b, img_b, t)

    scatter_pass(acc_of[1], core_of[1], half_of[1], part_of[1], 1)
    scatter_pass(acc_of[2], core_of[2], half_of[2], part_of[2], 6)

    @pl.loop(0, terms, unroll=4)
    def _(t):
        grow(2, 0, img_a, img_b, t)

    put_plain(0, 0, vec)
    put_plain(1, 0, cor)
    put_cross(2, 0, vec, cor)
    scatter_start(mats.at[0], core_m.at[0], 2)
    level_near = level_of(1)
    shard = scatter_end(part_of[1], 1)
    correct(1, level_near, shard)
    gather_start(cor_of[1], 2)
    shard = scatter_end(part_of[2], 6)
    correct(2, level_near, shard)
    gather_start(cor_of[2], 3)

    @pl.loop(0, terms, unroll=4)
    def _(t):
        grow(0, 1, img_a, img_a, t)

    put_plain(0, 1, vec)
    scatter_start(mats.at[1, 0], core_m.at[1, 0], 3)
    gather_pass(cor_of[1], 2)
    gather_end(cor_of[1], 2)

    @pl.loop(0, middle, unroll=True)
    def _(t):
        part_one(t, cor, img_b, acc_b)

    gather_pass(cor_of[2], 3)

    @pl.loop(middle, terms, unroll=True)
    def _(t):
        part_one(t, cor, img_b, acc_b)


    def overlaps(k):
        wide, corr = vec[k].astype(F32), cor[k].astype(F32)
        return fold(wide * corr), fold(corr * corr)

    plain = [overlaps(0), overlaps(1)]
    gather_end(cor_of[2], 3)
    tag_out[...] = jnp.broadcast_to(level_near, (8, half))
    scatter_pass(mats.at[0], core_m.at[0], half_m.at[0], part_m, 2)

    @pl.loop(0, terms, unroll=True)
    def _(t):
        part_two(t, cor, img_b, acc_b)

    plain[1] = [one + two for one, two in zip(plain[1], overlaps(2))]
    levels = [level_zero, level_near]
    sides = [(h_zero, a_zero), (h_near, a_near)]
    gathered = [jnp.zeros((1, half), F32)] * 6
    for team in range(2):
        level, (h_row, a_row) = levels[team], sides[team]
        vc, cc = plain[team]
        vhc = chc = jnp.zeros((1, half), F32)
        for k in teams[team]:
            summed = acc_b[k]
            vhc = vhc + fold(vec[k].astype(F32) * summed)
            chc = chc + fold(cor[k].astype(F32) * summed)
        here = [
            a_row * each,
            h_row,
            (vc + level * a_row) * each,
            (cc + level * (2.0 * vc + level * a_row)) * each,
            vhc + level * h_row,
            chc + level * (2.0 * vhc + level * h_row),
        ]
        gathered = [one + two for one, two in zip(gathered, here)]
    scalar_start(2, 1, row_of(gathered))
    scatter_pass(mats.at[1, 0], core_m.at[1, 0], half_m.at[1, 0], part_n.at[0], 3)

    @pl.loop(0, terms, unroll=True)
    def _(t):
        grow(1, 1, img_b, img_b, t)

    put_plain(1, 1, cor)
    scatter_start(mats.at[1, 1], core_m.at[1, 1], 4)

    @pl.loop(0, terms, unroll=4)
    def _(t):
        grow(2, 1, img_a, img_b, t)

    put_cross(2, 1, vec, cor)
    scatter_start(mats.at[1, 2], core_m.at[1, 2], 5)
    scatter_pass(mats.at[1, 1], core_m.at[1, 1], half_m.at[1, 1], part_n.at[1], 4)
    scalar_start(2, 2, scalar_wait(2, 1))
    to_owner = [
        send(cor.at[2], cor_got, one_send.at[2], one_recv.at[2], down, lane),
        send(tag_out, tag_in, one_send.at[3], one_recv.at[3], down, lane),
    ]
    start_one(*to_owner)
    scatter_pass(mats.at[1, 2], core_m.at[1, 2], half_m.at[1, 2], part_n.at[2], 5)
    scalar_start(2, 0, scalar_wait(2, 2))
    stay = scatter_end(part_m, 2)
    count = stay.shape[1]
    for q in range(3):
        hop_out[q * count:(q + 1) * count] = scatter_end(part_n.at[q], 3 + q)
    hop_out[3 * count:] = jnp.broadcast_to(level_near, (8, half))
    hop = send(hop_out, hop_in, one_send.at[1], one_recv.at[1], up, lane)
    start_one(hop)
    whole = column_of(scalar_wait(2, 0))
    a11, h11, v_u, u_u, v_hu, u_hu = [whole[q:q + 1] for q in range(6)]
    mean = h11 / a11
    a12 = v_u - mean * a11
    a22 = u_u - mean * (2.0 * v_u - mean * a11)
    h12 = v_hu - mean * h11
    h22 = u_hu - mean * (2.0 * v_hu - mean * h11)
    quad_a = a11 * a22 - a12 * a12
    quad_b = h11 * a22 + h22 * a11 - 2.0 * h12 * a12
    quad_c = h11 * h22 - h12 * h12
    lowest = (quad_b - jnp.sqrt(jnp.maximum(quad_b * quad_b - 4.0 * quad_a * quad_c, 0.0))) / (
        2.0 * quad_a
    )
    ratio = (lowest * a11 - h11) / (h12 - lowest * a12)
    first_coef = lax.rsqrt(a11 + 2.0 * ratio * a12 + ratio * ratio * a22)
    second_coef = ratio * first_coef

    def weigh(coef, parts):
        return coef * coef * parts[0] + coef * second_coef * parts[2] + second_coef * second_coef * parts[1]

    coefs = [first_coef + second_coef * (level - mean) for level in levels]
    stay = weigh(coefs[0], [stay[q] for q in range(3)])
    hop.wait_recv()
    coef_last = first_coef + second_coef * (hop_in[3 * count:3 * count + 1, 0:1] - mean)
    come = weigh(coef_last, [hop_in[q * count:(q + 1) * count] for q in range(3)])
    piled = folded.at[pl.ds(0, 3 * half)]
    rows(piled, (c * xs + x) * count, count)[...] = stay + come
    gather_start(piled, 4)
    for copy in to_owner:
        copy.wait_recv()
    coefs.append(first_coef + second_coef * (tag_in[0:1, 0:1] - mean))
    rows_last = jnp.where(me + 2 < ns, left_dims[lax.rem(me + 2, ns)], 0)
    row = lax.broadcasted_iota(jnp.int32, (width, width), 0)
    col = lax.broadcasted_iota(jnp.int32, (width, width), 1)
    last = jnp.where((row < rows_last) & (col < cols_own), psi[2].astype(F32), 0.0)
    pairs = [(vec[k].astype(F32), cor[k].astype(F32)) for k in range(2)] + [(last, cor_got[...].astype(F32))]
    for k, (wide, corr) in enumerate(pairs):
        ns_mine[k] = (coefs[k] * wide + second_coef * corr).astype(BF16)
    tail = lax.broadcasted_iota(jnp.int32, (8, half), 0)
    live = jnp.broadcast_to(rows_own, (8, half)).astype(F32)
    folded[3 * half:] = jnp.where(tail == 0, live, lowest)
    state_copy = load(ns_mine, state_hbm, 7)
    state_copy.start()
    gather_pass(piled, 4)
    gather_end(piled, 4)
    folded_copy = load(folded, folded_hbm, 8)
    folded_copy.start()
    send(pack_l, got_l, pack_send.at[0], pack_recv.at[0, 0], down, lane).wait_send()
    send(pack_r, got_r, pack_send.at[1], pack_recv.at[1, 0], up, lane).wait_send()
    for copy in waits:
        copy.wait_send()
    state_copy.wait()
    folded_copy.wait()


def sign_kernel(half, folded, state_hbm, new_state_hbm, kept, energy, state, sem):
    width = 2 * half
    into = pltpu.make_async_copy(state_hbm, state, sem.at[0])
    into.start()
    row = lax.broadcasted_iota(jnp.int32, (width, width), 0)
    col = lax.broadcasted_iota(jnp.int32, (width, width), 1)
    identity = jnp.where(row == col, 1.0, 0.0).astype(F32)
    live = folded[3 * half:3 * half + 1, 0:1]
    energy[...] = folded[3 * half + 1:3 * half + 2, 0:1]
    corner = folded[half:width]
    density = jnp.concatenate([
        jnp.concatenate([folded[:half], corner], axis=1),
        jnp.concatenate([corner.T, folded[width:3 * half]], axis=1),
    ], axis=0)
    inside = (row.astype(F32) < live) & (col.astype(F32) < live)
    density = jnp.where(inside, density, 0.0)
    trace = jnp.sum(jnp.sum(density * identity, axis=0, keepdims=True), axis=1, keepdims=True)
    shifted = density - (trace / live) * identity
    square = jnp.sum(jnp.sum(shifted * shifted, axis=0, keepdims=True), axis=1, keepdims=True)
    kept[...] = shifted / jnp.sqrt(square)
    out = pltpu.make_async_copy(state, new_state_hbm, sem.at[1])

    def step():
        current = kept[...]
        high, low = halves(current)
        stacked = jnp.concatenate([high, low, high], axis=0)
        for first in range(0, width, half):
            block = slice(first, first + half)
            squared = dot(beside(high[block], low[block]), stacked)
            cubed = dot(beside(*halves(squared)), stacked)
            kept[block] = 1.5 * current[block] - 0.5 * cubed

    pl.loop(0, SIGN_STEPS // 2)(lambda _: step())
    into.wait()
    out.start()
    pl.loop(SIGN_STEPS // 2, SIGN_STEPS)(lambda _: step())
    kept[...] = 0.5 * (identity + kept[...])
    out.wait()


def per_device(zs, ns, tg, psi, left_ops, right_ops, left_dims, right_dims):
    terms, width = left_ops.shape[0], left_ops.shape[-1]
    half, xs = width // 2, tg // CORES
    quarter, ys = half // xs, ns // zs
    tall = 3 * half
    share = tall // 2 // xs
    most = max(tg, zs, ys)
    vmem, hbm = pl.BlockSpec(memory_space=pltpu.VMEM), pl.BlockSpec(memory_space=pltpu.HBM)
    dma = pltpu.SemaphoreType.DMA
    state, folded = pl.pallas_call(
        functools.partial(kernel, (ns, zs, tg, terms, width)),
        out_shape=(
            jax.ShapeDtypeStruct((3, width, width), BF16),
            jax.ShapeDtypeStruct((tall + 8, half), F32),
        ),
        in_specs=[hbm] * 5,
        out_specs=(hbm, hbm),
        scratch_shapes=[pltpu.SMEM((ns,), jnp.int32)] * 2
        + [pltpu.VMEM((3, width, width), BF16)]
        + [pltpu.VMEM((terms, width, width), BF16)] * 6
        + [pltpu.VMEM((terms, width + 8, half), BF16)] * 4
        + [pltpu.VMEM((width, width), BF16)]
        + [pltpu.VMEM((3, width, width), BF16)] * 2
        + [pltpu.VMEM((terms, 3, width, width), BF16)] * 2
        + [pltpu.VMEM((3, width, width), F32)] * 2
        + [pltpu.VMEM((3, half, width), F32)] * 2
        + [pltpu.VMEM((3, xs, 1, quarter, width), F32)]
        + [pltpu.VMEM((2, 3, width, width), F32)]
        + [pltpu.VMEM((2, 3, tall, half), F32)]
        + [pltpu.VMEM((2, 3, tall // 2, half), F32)] * 2
        + [pltpu.VMEM((xs, 3, share, half), F32)]
        + [pltpu.VMEM((3, xs, share, half), F32)]
        + [pltpu.VMEM((3 * share + 8, half), F32)] * 2
        + [pltpu.VMEM((tall + 8, half), F32)]
        + [pltpu.VMEM((3, 3, most, 1, half), F32)]
        + [pltpu.VMEM((3, width, width), BF16), pltpu.VMEM((width, width), BF16)]
        + [pltpu.VMEM((8, half), F32)] * 2
        + [dma((9,)), dma((2,)), dma((2, terms)), dma((4,)), dma((4,))]
        + [dma((7,)), dma((7, xs)), dma((7,)), dma((7,)), dma((5,)), dma((5,)), dma((5,)), dma((5, xs))]
        + [dma((5,))] * 2
        + [pltpu.SemaphoreType.REGULAR((2, max(zs // 2, ys // 2, 2) - 1, 2))],
        compiler_params=pltpu.CompilerParams(
            collective_id=0, has_side_effects=True, vmem_limit_bytes=67043328
        ),
    )(left_dims, right_dims, psi[0], left_ops[:, 0], right_ops[:, 0])
    new_state, kept, energy = pl.pallas_call(
        functools.partial(sign_kernel, half),
        out_shape=(
            jax.ShapeDtypeStruct((3, width, width), BF16),
            jax.ShapeDtypeStruct((width, width), F32),
            jax.ShapeDtypeStruct((1, 1), F32),
        ),
        in_specs=[vmem, hbm],
        out_specs=(hbm, vmem, vmem),
        scratch_shapes=[pltpu.VMEM((3, width, width), BF16), dma((2,))],
    )(folded, state)
    return new_state[None], kept[None], energy[0, 0]


def solution(mesh):
    ns, tg = mesh.shape["sec"], mesh.shape["term"]
    zs = ZSIZE if ns % ZSIZE == 0 and ns > ZSIZE else 2
    in_specs = (
        P("sec", None, None, None),
        P("term", "sec", None, None),
        P("term", "sec", None, None),
        P(),
        P(),
    )
    out_specs = (P("sec", None, None, None), P("sec", None, None), P())
    return jax.shard_map(
        functools.partial(per_device, zs, ns, tg),
        mesh=mesh, in_specs=in_specs, out_specs=out_specs, check_vma=False,
    )
```
